512 devices in a mesh: group: 16 (over y, z_hi), seq: 4 (over z_lo), tensor: 8 (over x, core).
Axes of the slice: x: 4, y: 4, z: 16 (z_hi: 4, z_lo: 4; z = z_hi * 4 + z_lo), core: 2. Of those that a mesh axis runs over, the one named last changes fastest.
Arguments:
- span_tokens: bfloat16 [16, 1024, 2048], P('group', 'seq', 'tensor'), may hold values from -6 to 6
- q_weight: bfloat16 [2048, 2048], P(None, 'tensor'), may hold values from -0.125 to 0.125
- kv_weight: bfloat16 [2048, 512], P(None, 'tensor'), may hold values from -0.125 to 0.125
- out_weight: bfloat16 [2048, 2048], P('tensor'), may hold values from -0.1875 to 0.1875
- kv_pool: bfloat16 [256, 128, 512], P('group', None, 'tensor'), may hold values from -55 to 55, as said below
- cache_lengths: int32 [16], replicated, may hold values from 128 to 8192, as said below
- slot_requests: int32 [16], replicated, may hold values from 0 to 15, as said below
- page_table: int32 [16, 16], replicated, may hold values from 0 to 255, as said below
Outputs:
- attended: bfloat16 [16, 1024, 2048], P('group', 'seq', 'tensor')
The draws below stay inside these ranges and needn't reach their ends.
Inputs may be any that keep to these rules, and one draw needn't show every extreme that they name: `slot_requests`: A permutation; slot j is processed by group j. `page_table`: no pool page is named twice. The window pages of the requests dealt to one group lie 1 in each group's pool. `cache_lengths`: multiples of 128. `kv_pool`: cached keys and values.
All inputs are finite; a program needn't handle non-finite values.
Results may differ from the reference program's by a relative error of at most 0.015.
Values may be sent and summed in bfloat16 or wider, within the bound.
A program may use at most 64 MiB of HBM per device.

```python
import jax
import jax.numpy as jnp
from jax import lax

D = 2048
H = 32
HD = 64
KVH = 4
WINDOW = 2048
PAGE = 128
SPAN = 1024
REQ_G = 1
REQUESTS = 16
KV_PER = 1
WP = 16
POOL_G = 16
CAP = 1
PAGES = 256
MAXP = 64
N_TENSOR = 8


def dealing(key):
    dealt_key = jax.random.fold_in(key, 11)
    slot_key, rotate_key, pool_key = jax.random.split(dealt_key, 3)
    group_count = REQUESTS // REQ_G
    slot_requests = jax.random.permutation(slot_key, REQUESTS).astype(jnp.int32)
    rotations = jax.random.randint(rotate_key, (group_count,), 0, group_count)
    pool_orders = jax.vmap(lambda sub_key: jax.random.permutation(sub_key, POOL_G))(jax.random.split(pool_key, group_count))
    slots = jnp.arange(REQUESTS, dtype=jnp.int32)
    target_group = slots // REQ_G
    within = slots % REQ_G
    entry_index = within[:, None] * WP + jnp.arange(WP, dtype=jnp.int32)[None, :]
    owner_group = (entry_index + rotations[target_group][:, None]) % group_count
    pool_place = pool_orders[owner_group, target_group[:, None] * CAP + entry_index // group_count]
    by_slot = (owner_group * POOL_G + pool_place).astype(jnp.int32)
    page_rows = jnp.zeros((REQUESTS, WP), jnp.int32).at[slot_requests].set(by_slot)
    return (slot_requests, page_rows)


def draw_slot_requests(key, part):
    return dealing(key)[0]


def draw_page_table(key, part):
    return dealing(key)[1]


def draw_cache_lengths(key, part):
    count_key, order_key = jax.random.split(jax.random.fold_in(key, 23))
    page_counts = jax.random.randint(count_key, (REQUESTS,), 1, MAXP + 1)
    order = jax.random.permutation(order_key, REQUESTS)
    page_counts = page_counts.at[order[0]].set(MAXP).at[order[1]].set(1)
    return (page_counts * PAGE).astype(jnp.int32)


def draw_kv_pool(key, part):
    value_key = jax.random.fold_in(jax.random.fold_in(key, 37), 0)
    shape_all = (PAGES, PAGE, 2 * KVH * HD)
    values = jnp.clip(jax.random.normal(value_key, shape_all, jnp.float32), -6.0, 6.0)
    return values.astype(jnp.bfloat16)


def spiked(entries, stream_key, source, target, blocks, factor):
    owner, partner = [(jnp.arange(entries.shape[position]) // (entries.shape[position] // blocks)).reshape([-1 if axis == position else 1 for axis in range(entries.ndim)]) for position in (source, target)]
    chosen = jax.random.permutation(stream_key, blocks)[partner]
    strong = (owner == chosen) | (owner == (partner + blocks // 2) % blocks)
    return jnp.where(strong, factor * entries, entries)


def levels(key, shape, shards, least, top_value):
    factor_of = 1.0
    for dim, blocks in shards:
        draws = jax.random.uniform(jax.random.fold_in(jax.random.fold_in(key, 6), dim), (blocks,), jnp.float32, least / len(shards), top_value / len(shards))
        factor_of = factor_of * jnp.repeat(jnp.exp(draws), shape[dim] // blocks).reshape((-1,) + (1,) * (len(shape) - 1 - dim))
    return factor_of


def bell_draw(stream_key, dims, deviation, limit, cuts=(), kind=jnp.bfloat16):
    loudness = levels(stream_key, dims, cuts, -0.22, 0.18) if cuts else 1.0
    values = jax.random.normal(stream_key, dims, jnp.float32) * deviation * loudness
    return jnp.minimum(jnp.maximum(values, -limit), limit).astype(kind)


def noise_with(rng, extent, spread, reach, pieces, heavy, kind=jnp.bfloat16):
    drawn = spread * jax.random.normal(rng, extent, jnp.float32)
    if pieces:
        drawn = drawn * levels(rng, extent, pieces, -0.22, 0.18)
    return jnp.clip(spiked(drawn, jax.random.fold_in(rng, 3), *heavy), -reach, reach).astype(kind)


def setup_inputs(seed: int = 0) -> dict:
    key_list = jax.random.split(jax.random.key(seed), 9)
    span_tokens = bell_draw(key_list[0], (REQUESTS, SPAN, D), 1.0, 6.0, ((0, 16), (1, 4), (2, 8)))
    q_weight = bell_draw(key_list[1], (D, H * HD), D ** -0.5, 0.125, ((1, 8),))
    kv_weight = bell_draw(key_list[2], (D, 2 * KVH * HD), D ** -0.5, 0.125, ((1, 8),))
    out_weight = noise_with(key_list[3], (H * HD, D), (H * HD) ** -0.5, 0.1875, ((0, 8),), (0, 1, 8, 2.0))
    kv_pool = draw_kv_pool(jax.random.fold_in(key_list[8], 71), 0)
    cache_lengths = draw_cache_lengths(jax.random.fold_in(key_list[8], 71), 0)
    slot_requests = draw_slot_requests(jax.random.fold_in(key_list[8], 71), 0)
    page_table = draw_page_table(jax.random.fold_in(key_list[8], 71), 0)
    return dict(span_tokens=span_tokens, q_weight=q_weight, kv_weight=kv_weight, out_weight=out_weight, kv_pool=kv_pool, cache_lengths=cache_lengths, slot_requests=slot_requests, page_table=page_table)


def rotate(values, positions):
    half_dim = HD // 2
    frequency = jnp.power(jnp.float32(10000.0), -jnp.arange(half_dim, dtype=jnp.float32) / half_dim)
    angles = positions.astype(jnp.float32)[:, None] * frequency[None, :]
    cosine = jnp.cos(angles)[:, None, :]
    sine_part = jnp.sin(angles)[:, None, :]
    front_half = values[..., :half_dim]
    back_half = values[..., half_dim:]
    return jnp.concatenate([front_half * cosine - back_half * sine_part, back_half * cosine + front_half * sine_part], axis=-1)


def attend(block_q, block_k, block_v, base_pos):
    query_count = block_q.shape[0]
    key_count = block_k.shape[0]
    scores = jnp.einsum("tkgd,nkd->kgtn", block_q.astype(jnp.float32), block_k.astype(jnp.float32)) * (HD ** -0.5)
    query_at = jnp.arange(query_count, dtype=jnp.int32)[:, None]
    key_at = jnp.arange(key_count, dtype=jnp.int32)[None, :]
    allowed = (key_at > query_at) & (key_at <= query_at + WINDOW) & (base_pos + key_at >= 0)
    masked = jnp.where(allowed, scores, jnp.float32(-1e30))
    row_top = jnp.max(masked, axis=-1, keepdims=True)
    weights = jnp.where(allowed, jnp.exp(masked - row_top), jnp.float32(0.0))
    row_total = jnp.sum(weights, axis=-1)
    rounded = weights.astype(jnp.bfloat16)
    mixed_rows = jnp.einsum("kgtn,nkd->tkgd", rounded.astype(jnp.float32), block_v.astype(jnp.float32))
    mixed_rows = mixed_rows / jnp.transpose(row_total, (2, 0, 1))[..., None]
    return mixed_rows.astype(jnp.bfloat16).reshape(query_count, -1)


def reference(span_tokens, q_weight, kv_weight, out_weight, kv_pool, cache_lengths, slot_requests, page_table):
    block_len = min(128, SPAN)
    per_kv = H // KVH
    head_groups = N_TENSOR // 2

    def one_slot(slot_index):
        request = slot_requests[slot_index]
        length = cache_lengths[request]
        tokens = span_tokens[slot_index]
        positions = length + jnp.arange(SPAN, dtype=jnp.int32)
        queries = jnp.dot(tokens, q_weight, preferred_element_type=jnp.float32).reshape(SPAN, H, HD)
        queries = rotate(queries, positions).astype(jnp.bfloat16).reshape(SPAN, KVH, per_kv, HD)
        fresh_rows = jnp.dot(tokens, kv_weight, preferred_element_type=jnp.float32).reshape(SPAN, head_groups, 2, KV_PER, HD)
        new_keys = rotate(fresh_rows[:, :, 0].reshape(SPAN, KVH, HD), positions).astype(jnp.bfloat16)
        new_values = fresh_rows[:, :, 1].reshape(SPAN, KVH, HD).astype(jnp.bfloat16)
        page_rows = kv_pool[page_table[request]].reshape(WINDOW, head_groups, 2, KV_PER, HD)
        key_rows = jnp.concatenate([page_rows[:, :, 0].reshape(WINDOW, KVH, HD), new_keys], axis=0)
        value_rows = jnp.concatenate([page_rows[:, :, 1].reshape(WINDOW, KVH, HD), new_values], axis=0)

        def one_block(block_index):
            first_row = block_index * block_len
            block_q = lax.dynamic_slice_in_dim(queries, first_row, block_len, 0)
            block_k = lax.dynamic_slice_in_dim(key_rows, first_row, WINDOW + block_len, 0)
            block_v = lax.dynamic_slice_in_dim(value_rows, first_row, WINDOW + block_len, 0)
            return attend(block_q, block_k, block_v, length - WINDOW + first_row)

        blocks = lax.map(one_block, jnp.arange(SPAN // block_len, dtype=jnp.int32))
        heads_out = blocks.reshape(SPAN, N_TENSOR, H * HD // N_TENSOR)
        out_groups = out_weight.reshape(N_TENSOR, H * HD // N_TENSOR, D)
        partial_value = jnp.einsum("tgk,gkd->gtd", heads_out.astype(jnp.float32), out_groups.astype(jnp.float32)).astype(jnp.bfloat16)
        return jnp.sum(partial_value.astype(jnp.float32), axis=0).astype(jnp.bfloat16)

    return lax.map(one_slot, jnp.arange(REQUESTS, dtype=jnp.int32))
```

```python
import functools

import jax
import jax.numpy as jnp
from jax import lax
from jax.experimental import pallas as pl
from jax.experimental.pallas import tpu as pltpu
from jax.sharding import PartitionSpec as P

HD = 64
WINDOW = 2048
PAGE = 128
MESH = pl.DeviceIdType.MESH
NEG = -1e30
FLOOR = -1e20
F32 = jnp.float32
BF16 = jnp.bfloat16


def layer_kernel(
    wanted_ref, place_ref, length_ref, cos_ref, sin_ref, x_ref, qw_ref, kvw_ref, ow_ref, pool_ref,
    out_ref,
    xs, outp, kv, fresh, qacc, kvacc, qt, acc, top, tot, thr_ref, part, mine, pairin, bsum, landed, relay,
    x_send, x_recv, xf_send, xf_recv, p_send, p_recv, pf_send, pf_recv,
    n_send, n_recv, nf_send, nf_recv, r_send, r_recv, s_send, s_recv,
):
    group = lax.axis_index("group")
    seq = lax.axis_index("seq")
    tensor = lax.axis_index("tensor")
    chip = tensor // 2
    core = tensor % 2
    gy = group // 4
    gz = group % 4
    partner = {"tensor": chip * 2 + (1 - core)}

    def chip_at(d):
        return {"tensor": ((chip + d) % 4) * 2 + core}

    def group_to(s):
        dy, dz = s // 4, s % 4
        return ((gy + dy) % 4) * 4 + (gz + dz) % 4

    def group_from(s):
        dy, dz = s // 4, s % 4
        return ((gy - dy + 4) % 4) * 4 + (gz - dz + 4) % 4

    def page_dev(s):
        if s % 4 == 2:
            return {"group": group_to(s), "seq": seq + 1 - 2 * (seq % 2)}
        return {"group": group_to(s)}

    def remote(src, dst, ss, rs, dev):
        return pltpu.make_async_remote_copy(
            src_ref=src, dst_ref=dst, send_sem=ss, recv_sem=rs, device_id=dev, device_id_type=MESH
        )

    barrier = pltpu.get_barrier_semaphore()
    for s in range(1, 16):
        pl.semaphore_signal(barrier, inc=1, device_id=page_dev(s), device_id_type=MESH)
    for b in range(1, 4):
        pl.semaphore_signal(barrier, inc=1, device_id={"seq": (seq + b) % 4}, device_id_type=MESH)
    for d in range(1, 4):
        if d != 2:
            pl.semaphore_signal(barrier, inc=1, device_id=chip_at(d), device_id_type=MESH)
    pl.semaphore_signal(barrier, inc=1, device_id=partner, device_id_type=MESH)

    for s in range(1, 16):
        outp[s - 1] = pool_ref[wanted_ref[group_to(s)]]
    kv[core, 0] = pool_ref[wanted_ref[group]]
    thr_ref[...] = jnp.maximum(
        lax.broadcasted_iota(jnp.int32, (1, 256), 1) + seq * 256, WINDOW - 1 - length_ref[0]
    )
    for h in range(4):
        acc[h] = jnp.zeros((HD, 256), F32)
        top[h] = jnp.full((1, 256), FLOOR, F32)
        tot[h] = jnp.zeros((1, 256), F32)

    pl.semaphore_wait(barrier, 21)

    first = {d: remote(x_ref, xs.at[0, 4 - d], x_send.at[d], x_recv.at[4 - d], chip_at(d)) for d in (1, 3)}
    own_x = remote(x_ref, xs.at[1, 0], xf_send.at[0], xf_recv.at[0], partner)
    for d in (1, 3):
        first[d].start()
    own_x.start()
    order = [1, 3, 4, 8, 12, 5, 7, 9, 11, 13, 15, 2, 6, 10, 14]
    pages = {
        s: remote(outp.at[s - 1], kv.at[core, s], p_send.at[s], p_recv.at[s], page_dev(s)) for s in order
    }
    for s in (2, 6, 10, 14, 1, 3, 5, 7, 9, 11, 13, 15, 4, 8, 12):
        pages[s].start()
    pagef = {
        s: remote(kv.at[core, s], kv.at[core, s], pf_send.at[s], pf_recv.at[s], partner) for s in range(16)
    }
    pagef[0].start()

    def project(p, d):
        block = x_ref[...] if (p, d) == (0, 0) else xs[p, d]
        t = ((chip + d) % 4) * 2 + (core if p == 0 else 1 - core)
        rows = pl.ds(pl.multiple_of(t * 256, 256), 256)
        q = jnp.dot(block, qw_ref[rows, :], preferred_element_type=F32)
        f = lax.dot_general(kvw_ref[:, rows], block, (((1,), (1,)), ((), ())), preferred_element_type=F32)
        if (p, d) == (0, 0):
            qacc[...] = q
            kvacc[...] = f
        else:
            qacc[...] += q
            kvacc[...] += f

    project(0, 0)
    xf = {d: remote(xs.at[0, d], xs.at[1, d], xf_send.at[d], xf_recv.at[d], partner) for d in (1, 2, 3)}
    from_slot = 3 - 2 * core
    on = {"tensor": ((chip + 1 + 2 * core) % 4) * 2 + core}
    first[3].wait_recv()
    first[1].wait_recv()
    second = remote(xs.at[0, from_slot], xs.at[0, 2], x_send.at[2], x_recv.at[2], on)
    second.start()
    xf[1].start()
    xf[3].start()
    own_x.wait_recv()
    project(1, 0)
    project(0, 1)
    project(0, 3)
    xf[1].wait_recv()
    project(1, 1)
    xf[3].wait_recv()
    project(1, 3)
    second.wait_recv()
    xf[2].start()
    project(0, 2)
    xf[2].wait_recv()
    project(1, 2)

    is_key = jnp.where(core == 0, 1.0, 0.0).astype(F32)
    cos = cos_ref[...]
    sin = sin_ref[...]
    kcos = cos * is_key + (1.0 - is_key)
    ksin = sin * is_key
    a = kvacc[:32, :]
    b = kvacc[32:, :]
    fresh[core, 0] = jnp.concatenate([a * kcos - b * ksin, b * kcos + a * ksin], axis=0).astype(BF16)
    for step in range(1, 4):
        @pl.when(seq + step < 4)
        def _():
            remote(
                fresh.at[core, 0], fresh.at[core, step], n_send.at[step], n_recv.at[step], {"seq": (seq + step) % 4}
            ).start()
    newf = {
        i: remote(fresh.at[core, i], fresh.at[core, i], nf_send.at[i], nf_recv.at[i], partner) for i in range(4)
    }
    newf[0].start()
    for h in range(4):
        w = qacc[:, h * HD:(h + 1) * HD].T
        a = w[:32, :] * 0.125
        b = w[32:, :] * 0.125
        qt[h] = jnp.concatenate([a * cos - b * sin, b * cos + a * sin], axis=0).astype(BF16)

    def fold(keys, values, mask):
        kb = keys.T

        def head(h, carry):
            s = jnp.dot(kb, qt[h], preferred_element_type=F32)
            s = mask(s)
            old = top[h]
            new = jnp.maximum(old, jnp.max(s, axis=0, keepdims=True))
            p = jnp.exp(s - new)
            alpha = jnp.exp(old - new)
            top[h] = new
            tot[h] = tot[h] * alpha + jnp.sum(p, axis=0, keepdims=True)
            acc[h] = acc[h] * alpha + jnp.dot(values, p.astype(BF16), preferred_element_type=F32)
            return carry

        lax.fori_loop(0, 4, head, 0)

    row = lax.broadcasted_iota(jnp.int32, (PAGE, 256), 0)

    def fold_pages(slots):
        def mask(s):
            pieces = []
            for i, slot in enumerate(slots):
                low = thr_ref[...] - place_ref[group_from(slot)] * PAGE
                pieces.append(jnp.where(row > low, s[i * PAGE:(i + 1) * PAGE], NEG))
            return jnp.concatenate(pieces, axis=0)

        fold(
            jnp.concatenate([kv[0, s] for s in slots], axis=1),
            jnp.concatenate([kv[1, s] for s in slots], axis=1),
            mask,
        )

    def take(slots):
        for s in slots:
            pages[s].wait_recv()
            pagef[s].start()

    def ready(slots):
        for s in slots:
            remote(kv.at[core, s], kv.at[1 - core, s], pf_send.at[s], pf_recv.at[s], partner).wait_recv()

    causal = lax.broadcasted_iota(jnp.int32, (256, 256), 0) <= lax.broadcasted_iota(jnp.int32, (256, 256), 1)

    def new_ready(i):
        remote(fresh.at[core, i], fresh.at[1 - core, i], nf_send.at[i], nf_recv.at[i], partner).wait_recv()

    new_ready(0)
    fold(fresh[0, 0], fresh[1, 0], lambda s: jnp.where(causal, s, NEG))
    c0, c1, c2, c3 = [0, 4, 8, 12], [1, 3, 5, 7], [9, 11, 13, 15], [2, 6, 10, 14]
    take(c0[1:])
    take(c1)
    ready(c0)
    fold_pages(c0)
    take(c2)
    ready(c1)
    fold_pages(c1)
    take(c3)
    ready(c2)
    fold_pages(c2)
    for step in range(1, 4):
        @pl.when(seq >= step)
        def _():
            remote(
                fresh.at[core, 0], fresh.at[core, step], n_send.at[step], n_recv.at[step], {"seq": (seq + step) % 4}
            ).wait_recv()
            newf[step].start()
    ready(c3)
    fold_pages(c3)
    for step in range(1, 4):
        @pl.when(seq >= step)
        def _():
            new_ready(step)
            fold(fresh[0, step], fresh[1, step], lambda s: s)

    heads = jnp.concatenate([(acc[h] / tot[h]).T.astype(BF16) for h in range(4)], axis=1)

    def partial_for(d, c):
        cols = pl.ds(pl.multiple_of((((chip + d) % 4) * 2 + c) * 256, 256), 256)
        return jnp.dot(heads, ow_ref[:, cols], preferred_element_type=F32).astype(BF16)

    near = 1 + 2 * core
    far = 3 - 2 * core
    rs = {}
    for d in (2, 1, 3, 0):
        part[d] = partial_for(d, 1 - core)
        rs[d] = remote(part.at[d], pairin.at[d], r_send.at[d], r_recv.at[d], partner)
        rs[d].start()
    for d in (2, 1, 3, 0):
        mine[d] = partial_for(d, core)
    up = {"tensor": ((chip + near) % 4) * 2 + core}
    down = {"tensor": ((chip + far) % 4) * 2 + core}
    rs[2].wait_recv()
    bsum[0] = (mine[2].astype(F32) + pairin[2].astype(F32)).astype(BF16)
    s2 = remote(bsum.at[0], landed.at[0], s_send.at[0], s_recv.at[0], up)
    s2.start()
    rs[1].wait_recv()
    rs[3].wait_recv()
    bsum[1] = (mine[far].astype(F32) + pairin[far].astype(F32)).astype(BF16)
    s3 = remote(bsum.at[1], landed.at[1], s_send.at[1], s_recv.at[1], down)
    s3.start()
    rs[0].wait_recv()
    nearsum = mine[near].astype(F32) + pairin[near].astype(F32)
    s2.wait_recv()
    relay[...] = (nearsum + landed[0].astype(F32)).astype(BF16)
    s1 = remote(relay, landed.at[2], s_send.at[2], s_recv.at[2], up)
    s1.start()
    total = mine[0].astype(F32) + pairin[0].astype(F32)
    s3.wait_recv()
    total = total + landed[1].astype(F32)
    s1.wait_recv()
    out_ref[...] = (total + landed[2].astype(F32)).astype(BF16)

    for copy in [first[1], first[3], own_x, second, xf[1], xf[2], xf[3], s1, s2, s3]:
        copy.wait_send()
    for s in range(1, 16):
        pages[s].wait_send()
    for s in range(16):
        pagef[s].wait_send()
    for d in range(4):
        rs[d].wait_send()
    newf[0].wait_send()
    for step in range(1, 4):
        @pl.when(seq >= step)
        def _():
            newf[step].wait_send()

        @pl.when(seq + step < 4)
        def _():
            remote(
                fresh.at[core, 0], fresh.at[core, step], n_send.at[step], n_recv.at[step], {"seq": (seq + step) % 4}
            ).wait_send()


def shards(
    span_tokens, q_weight, kv_weight, out_weight, kv_pool, cache_lengths, slot_requests, page_table
):
    group_id = lax.axis_index("group")
    seq_id = lax.axis_index("seq")
    lane = jnp.arange(16, dtype=jnp.int32)
    picked = (slot_requests[:, None] == lane[None, :]).astype(jnp.int32)
    ids = jnp.sum(picked[:, :, None] * page_table[None, :, :], axis=1)
    wanted = jnp.sum(jnp.where(ids // 16 == group_id, ids % 16, 0), axis=1)
    here = (lane == group_id).astype(jnp.int32)
    my_pick = jnp.sum(picked * here[:, None], axis=0)
    my_ids = jnp.sum(my_pick[:, None] * page_table, axis=0)
    place = jnp.sum(jnp.where(my_ids[None, :] // 16 == lane[:, None], lane[None, :], 0), axis=1)
    length = jnp.sum(my_pick * cache_lengths)
    half_dim = HD // 2
    frequency = jnp.power(F32(10000.0), -jnp.arange(half_dim, dtype=F32) / half_dim)
    positions = length + seq_id * 256 + jnp.arange(256, dtype=jnp.int32)
    angles = frequency[:, None] * positions.astype(F32)[None, :]
    smem = pl.BlockSpec(memory_space=pltpu.SMEM)
    vmem = pl.BlockSpec(memory_space=pltpu.VMEM)
    dma = pltpu.SemaphoreType.DMA
    out = pl.pallas_call(
        layer_kernel,
        out_shape=jax.ShapeDtypeStruct((256, 256), BF16),
        in_specs=[smem] * 3 + [vmem] * 7,
        out_specs=vmem,
        scratch_shapes=[
            pltpu.VMEM((2, 4, 256, 256), BF16),
            pltpu.VMEM((15, HD, PAGE), BF16),
            pltpu.VMEM((2, 16, HD, PAGE), BF16),
            pltpu.VMEM((2, 4, HD, 256), BF16),
            pltpu.VMEM((256, 256), F32),
            pltpu.VMEM((HD, 256), F32),
            pltpu.VMEM((4, HD, 256), BF16),
            pltpu.VMEM((4, HD, 256), F32),
            pltpu.VMEM((4, 1, 256), F32),
            pltpu.VMEM((4, 1, 256), F32),
            pltpu.VMEM((1, 256), jnp.int32),
            pltpu.VMEM((4, 256, 256), BF16),
            pltpu.VMEM((4, 256, 256), BF16),
            pltpu.VMEM((4, 256, 256), BF16),
            pltpu.VMEM((2, 256, 256), BF16),
            pltpu.VMEM((3, 256, 256), BF16),
            pltpu.VMEM((256, 256), BF16),
            dma((4,)), dma((4,)), dma((4,)), dma((4,)),
            dma((16,)), dma((16,)), dma((16,)), dma((16,)),
            dma((4,)), dma((4,)), dma((4,)), dma((4,)),
            dma((4,)), dma((4,)), dma((3,)), dma((3,)),
        ],
        compiler_params=pltpu.CompilerParams(
            collective_id=0, has_side_effects=True, vmem_limit_bytes=48 * 1024 * 1024
        ),
    )(
        wanted, place, length.reshape(1), jnp.cos(angles), jnp.sin(angles),
        span_tokens.reshape(256, 256), q_weight, kv_weight.T, out_weight, jnp.swapaxes(kv_pool, 1, 2),
    )
    return out.reshape(1, 256, 256)


def solution(mesh):
    placed = (
        P("group", "seq", "tensor"),
        P(None, "tensor"),
        P(None, "tensor"),
        P("tensor", None),
        P("group", None, "tensor"),
        P(),
        P(),
        P(),
    )
    return jax.shard_map(
        shards, mesh=mesh, in_specs=placed, out_specs=P("group", "seq", "tensor"), check_vma=False
    )
```

```python
import functools

import jax
import jax.numpy as jnp
from jax import lax
from jax.experimental import pallas as pl
from jax.experimental.pallas import tpu as pltpu
from jax.sharding import PartitionSpec as P

HD = 64
WINDOW = 2048
PAGE = 128
MESH = pl.DeviceIdType.MESH
NEG = -1e30
FLOOR = -1e20
F32 = jnp.float32
BF16 = jnp.bfloat16


def layer_kernel(
    slots_ref, lengths_ref, table_ref, freq_ref, x_hbm, qw_hbm, kvw_hbm, ow_hbm, pool_hbm,
    out_ref,
    x_ref, qw_ref, kvw_ref, ow_ref, pool_ref, place_ref, load_sem, xs, outp, kv, fresh, qacc, kvacc, qt, acc, top, tot, thr_ref, cos_ref, sin_ref, part, mine, pairin, bsum, landed, relay,
    x_send, x_recv, xf_send, xf_recv, p_send, p_recv, pf_send, pf_recv,
    n_send, n_recv, nf_send, nf_recv, r_send, r_recv, s_send, s_recv,
):
    group = lax.axis_index("group")
    seq = lax.axis_index("seq")
    tensor = lax.axis_index("tensor")
    chip = tensor // 2
    core = tensor % 2
    gy = group // 4
    gz = group % 4
    partner = {"tensor": chip * 2 + (1 - core)}

    def chip_at(d):
        return {"tensor": ((chip + d) % 4) * 2 + core}

    def group_to(s):
        dy, dz = s // 4, s % 4
        return ((gy + dy) % 4) * 4 + (gz + dz) % 4

    def group_from(s):
        dy, dz = s // 4, s % 4
        return ((gy - dy + 4) % 4) * 4 + (gz - dz + 4) % 4

    def page_dev(s):
        if s % 4 == 2:
            return {"group": group_to(s), "seq": seq + 1 - 2 * (seq % 2)}
        return {"group": group_to(s)}

    def remote(src, dst, ss, rs, dev):
        return pltpu.make_async_remote_copy(
            src_ref=src, dst_ref=dst, send_sem=ss, recv_sem=rs, device_id=dev, device_id_type=MESH
        )

    barrier = pltpu.get_barrier_semaphore()
    for s in range(1, 16):
        pl.semaphore_signal(barrier, inc=1, device_id=page_dev(s), device_id_type=MESH)
    for b in range(1, 4):
        pl.semaphore_signal(barrier, inc=1, device_id={"seq": (seq + b) % 4}, device_id_type=MESH)
    for d in range(1, 4):
        if d != 2:
            pl.semaphore_signal(barrier, inc=1, device_id=chip_at(d), device_id_type=MESH)
    pl.semaphore_signal(barrier, inc=1, device_id=partner, device_id_type=MESH)

    loads = [
        pltpu.make_async_copy(src, dst, load_sem.at[i])
        for i, (src, dst) in enumerate(
            [(pool_hbm, pool_ref), (x_hbm, x_ref), (qw_hbm, qw_ref), (kvw_hbm, kvw_ref), (ow_hbm, ow_ref)]
        )
    ]
    for copy in loads:
        copy.start()

    mine_req = slots_ref[group]
    length = lengths_ref[mine_req]
    my_ids = [table_ref[mine_req, w] for w in range(16)]

    def find_place(s, carry):
        low = group_from(s) * 16
        at = 0
        for w in range(16):
            off = my_ids[w] - low
            at = at + jnp.where((off >= 0) & (off < 16), w, 0)
        place_ref[s] = at
        return carry

    lax.fori_loop(0, 16, find_place, 0)
    loads[0].wait()

    def pick(s, carry):
        req = slots_ref[group_to(s)]
        at = 0
        for w in range(16):
            off = table_ref[req, w] - group * 16
            at = at + jnp.where((off >= 0) & (off < 16), off, 0)
        outp[s] = pool_ref[at]
        return carry

    lax.fori_loop(0, 16, pick, 0)
    kv[core, 0] = outp[0]
    at_pos = lax.broadcasted_iota(jnp.int32, (32, 256), 1) + (length + seq * 256)
    angles = at_pos.astype(F32) * freq_ref[...]
    cos = jnp.cos(angles)
    sin = jnp.sin(angles)
    cos_ref[...] = cos
    sin_ref[...] = sin
    thr_ref[...] = jnp.maximum(
        lax.broadcasted_iota(jnp.int32, (1, 256), 1) + seq * 256, WINDOW - 1 - length
    )
    for h in range(4):
        acc[h] = jnp.zeros((HD, 256), F32)
        top[h] = jnp.full((1, 256), FLOOR, F32)
        tot[h] = jnp.zeros((1, 256), F32)

    loads[1].wait()
    pl.semaphore_wait(barrier, 21)

    first = {d: remote(x_ref, xs.at[0, 4 - d], x_send.at[d], x_recv.at[4 - d], chip_at(d)) for d in (1, 3)}
    own_x = remote(x_ref, xs.at[1, 0], xf_send.at[0], xf_recv.at[0], partner)
    for d in (1, 3):
        first[d].start()
    own_x.start()
    order = [1, 3, 4, 8, 12, 5, 7, 9, 11, 13, 15, 2, 6, 10, 14]
    pages = {
        s: remote(outp.at[s], kv.at[core, s], p_send.at[s], p_recv.at[s], page_dev(s)) for s in order
    }
    for s in (2, 6, 10, 14, 1, 3, 5, 7, 9, 11, 13, 15, 4, 8, 12):
        pages[s].start()
    pagef = {
        s: remote(kv.at[core, s], kv.at[core, s], pf_send.at[s], pf_recv.at[s], partner) for s in range(16)
    }
    pagef[0].start()
    loads[2].wait()
    loads[3].wait()

    def project(p, d):
        block = x_ref[...] if (p, d) == (0, 0) else xs[p, d]
        t = ((chip + d) % 4) * 2 + (core if p == 0 else 1 - core)
        rows = pl.ds(pl.multiple_of(t * 256, 256), 256)
        q = jnp.dot(block, qw_ref[rows, :], preferred_element_type=F32)
        f = lax.dot_general(kvw_ref[:, rows], block, (((1,), (1,)), ((), ())), preferred_element_type=F32)
        if (p, d) == (0, 0):
            qacc[...] = q
            kvacc[...] = f
        else:
            qacc[...] += q
            kvacc[...] += f

    project(0, 0)
    xf = {d: remote(xs.at[0, d], xs.at[1, d], xf_send.at[d], xf_recv.at[d], partner) for d in (1, 2, 3)}
    from_slot = 3 - 2 * core
    on = {"tensor": ((chip + 1 + 2 * core) % 4) * 2 + core}
    first[3].wait_recv()
    first[1].wait_recv()
    second = remote(xs.at[0, from_slot], xs.at[0, 2], x_send.at[2], x_recv.at[2], on)
    second.start()
    xf[1].start()
    xf[3].start()
    own_x.wait_recv()
    project(1, 0)
    project(0, 1)
    project(0, 3)
    xf[1].wait_recv()
    project(1, 1)
    xf[3].wait_recv()
    project(1, 3)
    second.wait_recv()
    xf[2].start()
    project(0, 2)
    xf[2].wait_recv()
    project(1, 2)

    is_key = jnp.where(core == 0, 1.0, 0.0).astype(F32)
    cos = cos_ref[...]
    sin = sin_ref[...]
    kcos = cos * is_key + (1.0 - is_key)
    ksin = sin * is_key
    a = kvacc[:32, :]
    b = kvacc[32:, :]
    fresh[core, 0] = jnp.concatenate([a * kcos - b * ksin, b * kcos + a * ksin], axis=0).astype(BF16)
    for step in range(1, 4):
        @pl.when(seq + step < 4)
        def _():
            remote(
                fresh.at[core, 0], fresh.at[core, step], n_send.at[step], n_recv.at[step], {"seq": (seq + step) % 4}
            ).start()
    newf = {
        i: remote(fresh.at[core, i], fresh.at[core, i], nf_send.at[i], nf_recv.at[i], partner) for i in range(4)
    }
    newf[0].start()
    for h in range(4):
        w = qacc[:, h * HD:(h + 1) * HD].T
        a = w[:32, :] * 0.125
        b = w[32:, :] * 0.125
        qt[h] = jnp.concatenate([a * cos - b * sin, b * cos + a * sin], axis=0).astype(BF16)

    def fold(keys, values, mask):
        kb = keys.T

        def head(h, carry):
            s = jnp.dot(kb, qt[h], preferred_element_type=F32)
            s = mask(s)
            old = top[h]
            new = jnp.maximum(old, jnp.max(s, axis=0, keepdims=True))
            p = jnp.exp(s - new)
            alpha = jnp.exp(old - new)
            top[h] = new
            tot[h] = tot[h] * alpha + jnp.sum(p, axis=0, keepdims=True)
            acc[h] = acc[h] * alpha + jnp.dot(values, p.astype(BF16), preferred_element_type=F32)
            return carry

        lax.fori_loop(0, 4, head, 0)

    row = lax.broadcasted_iota(jnp.int32, (PAGE, 256), 0)

    def fold_pages(slots):
        def mask(s):
            pieces = []
            for i, slot in enumerate(slots):
                low = thr_ref[...] - place_ref[slot] * PAGE
                pieces.append(jnp.where(row > low, s[i * PAGE:(i + 1) * PAGE], NEG))
            return jnp.concatenate(pieces, axis=0)

        fold(
            jnp.concatenate([kv[0, s] for s in slots], axis=1),
            jnp.concatenate([kv[1, s] for s in slots], axis=1),
            mask,
        )

    def take(slots):
        for s in slots:
            pages[s].wait_recv()
            pagef[s].start()

    def ready(slots):
        for s in slots:
            remote(kv.at[core, s], kv.at[1 - core, s], pf_send.at[s], pf_recv.at[s], partner).wait_recv()

    causal = lax.broadcasted_iota(jnp.int32, (256, 256), 0) <= lax.broadcasted_iota(jnp.int32, (256, 256), 1)

    def new_ready(i):
        remote(fresh.at[core, i], fresh.at[1 - core, i], nf_send.at[i], nf_recv.at[i], partner).wait_recv()

    new_ready(0)
    fold(fresh[0, 0], fresh[1, 0], lambda s: jnp.where(causal, s, NEG))
    c0, c1, c2, c3 = [0, 4, 8, 12], [1, 3, 5, 7], [9, 11, 13, 15], [2, 6, 10, 14]
    take(c0[1:])
    take(c1)
    ready(c0)
    fold_pages(c0)
    take(c2)
    ready(c1)
    fold_pages(c1)
    take(c3)
    ready(c2)
    fold_pages(c2)
    for step in range(1, 4):
        @pl.when(seq >= step)
        def _():
            remote(
                fresh.at[core, 0], fresh.at[core, step], n_send.at[step], n_recv.at[step], {"seq": (seq + step) % 4}
            ).wait_recv()
            newf[step].start()
    ready(c3)
    fold_pages(c3)
    for step in range(1, 4):
        @pl.when(seq >= step)
        def _():
            new_ready(step)
            fold(fresh[0, step], fresh[1, step], lambda s: s)

    loads[4].wait()
    heads = jnp.concatenate([(acc[h] / tot[h]).T.astype(BF16) for h in range(4)], axis=1)

    def partial_for(d, c):
        cols = pl.ds(pl.multiple_of((((chip + d) % 4) * 2 + c) * 256, 256), 256)
        return jnp.dot(heads, ow_ref[:, cols], preferred_element_type=F32).astype(BF16)

    near = 1 + 2 * core
    far = 3 - 2 * core
    rs = {}
    for d in (2, 1, 3, 0):
        part[d] = partial_for(d, 1 - core)
        rs[d] = remote(part.at[d], pairin.at[d], r_send.at[d], r_recv.at[d], partner)
        rs[d].start()
    for d in (2, 1, 3, 0):
        mine[d] = partial_for(d, core)
    up = {"tensor": ((chip + near) % 4) * 2 + core}
    down = {"tensor": ((chip + far) % 4) * 2 + core}
    rs[2].wait_recv()
    bsum[0] = (mine[2].astype(F32) + pairin[2].astype(F32)).astype(BF16)
    s2 = remote(bsum.at[0], landed.at[0], s_send.at[0], s_recv.at[0], up)
    s2.start()
    rs[1].wait_recv()
    rs[3].wait_recv()
    bsum[1] = (mine[far].astype(F32) + pairin[far].astype(F32)).astype(BF16)
    s3 = remote(bsum.at[1], landed.at[1], s_send.at[1], s_recv.at[1], down)
    s3.start()
    rs[0].wait_recv()
    nearsum = mine[near].astype(F32) + pairin[near].astype(F32)
    s2.wait_recv()
    relay[...] = (nearsum + landed[0].astype(F32)).astype(BF16)
    s1 = remote(relay, landed.at[2], s_send.at[2], s_recv.at[2], up)
    s1.start()
    total = mine[0].astype(F32) + pairin[0].astype(F32)
    s3.wait_recv()
    total = total + landed[1].astype(F32)
    s1.wait_recv()
    out_ref[...] = (total + landed[2].astype(F32)).astype(BF16)

    for copy in [first[1], first[3], own_x, second, xf[1], xf[2], xf[3], s1, s2, s3]:
        copy.wait_send()
    for s in range(1, 16):
        pages[s].wait_send()
    for s in range(16):
        pagef[s].wait_send()
    for d in range(4):
        rs[d].wait_send()
    newf[0].wait_send()
    for step in range(1, 4):
        @pl.when(seq >= step)
        def _():
            newf[step].wait_send()

        @pl.when(seq + step < 4)
        def _():
            remote(
                fresh.at[core, 0], fresh.at[core, step], n_send.at[step], n_recv.at[step], {"seq": (seq + step) % 4}
            ).wait_send()


def shards(
    span_tokens, q_weight, kv_weight, out_weight, kv_pool, cache_lengths, slot_requests, page_table
):
    half_dim = HD // 2
    frequency = jnp.power(F32(10000.0), -jnp.arange(half_dim, dtype=F32) / half_dim)
    frequency = jnp.broadcast_to(frequency[:, None], (half_dim, 256))
    smem = pl.BlockSpec(memory_space=pltpu.SMEM)
    vmem = pl.BlockSpec(memory_space=pltpu.VMEM)
    hbm = pl.BlockSpec(memory_space=pl.ANY)
    dma = pltpu.SemaphoreType.DMA
    out = pl.pallas_call(
        layer_kernel,
        out_shape=jax.ShapeDtypeStruct((256, 256), BF16),
        in_specs=[smem] * 3 + [vmem] + [hbm] * 5,
        out_specs=vmem,
        scratch_shapes=[
            pltpu.VMEM((256, 256), BF16),
            pltpu.VMEM((2048, 256), BF16),
            pltpu.VMEM((HD, 2048), BF16),
            pltpu.VMEM((256, 2048), BF16),
            pltpu.VMEM((16, HD, PAGE), BF16),
            pltpu.SMEM((16,), jnp.int32),
            dma((5,)),
            pltpu.VMEM((2, 4, 256, 256), BF16),
            pltpu.VMEM((16, HD, PAGE), BF16),
            pltpu.VMEM((2, 16, HD, PAGE), BF16),
            pltpu.VMEM((2, 4, HD, 256), BF16),
            pltpu.VMEM((256, 256), F32),
            pltpu.VMEM((HD, 256), F32),
            pltpu.VMEM((4, HD, 256), BF16),
            pltpu.VMEM((4, HD, 256), F32),
            pltpu.VMEM((4, 1, 256), F32),
            pltpu.VMEM((4, 1, 256), F32),
            pltpu.VMEM((1, 256), jnp.int32),
            pltpu.VMEM((32, 256), F32),
            pltpu.VMEM((32, 256), F32),
            pltpu.VMEM((4, 256, 256), BF16),
            pltpu.VMEM((4, 256, 256), BF16),
            pltpu.VMEM((4, 256, 256), BF16),
            pltpu.VMEM((2, 256, 256), BF16),
            pltpu.VMEM((3, 256, 256), BF16),
            pltpu.VMEM((256, 256), BF16),
            dma((4,)), dma((4,)), dma((4,)), dma((4,)),
            dma((16,)), dma((16,)), dma((16,)), dma((16,)),
            dma((4,)), dma((4,)), dma((4,)), dma((4,)),
            dma((4,)), dma((4,)), dma((3,)), dma((3,)),
        ],
        compiler_params=pltpu.CompilerParams(
            collective_id=0, has_side_effects=True, vmem_limit_bytes=63 * 1024 * 1024
        ),
    )(
        slot_requests, cache_lengths, page_table, frequency,
        span_tokens.reshape(256, 256), q_weight, kv_weight.T, out_weight, jnp.swapaxes(kv_pool, 1, 2),
    )
    return out.reshape(1, 256, 256)


def solution(mesh):
    placed = (
        P("group", "seq", "tensor"),
        P(None, "tensor"),
        P(None, "tensor"),
        P("tensor", None),
        P("group", None, "tensor"),
        P(),
        P(),
        P(),
    )
    return jax.shard_map(
        shards, mesh=mesh, in_specs=placed, out_specs=P("group", "seq", "tensor"), check_vma=False
    )
```

```python
import jax
import jax.numpy as jnp
import numpy as np
from jax import lax
from jax.experimental import pallas as pl
from jax.experimental.pallas import tpu as pltpu
from jax.sharding import PartitionSpec as P

HD = 64
WINDOW = 2048
PAGE = 128
MESH = pl.DeviceIdType.MESH
NEG = -1e30
FLOOR = -1e20
F32 = jnp.float32
BF16 = jnp.bfloat16


def layer_kernel(
    slots_ref, lengths_ref, table_ref, freq_ref, x_hbm, qw_hbm, kvw_hbm, ow_hbm, pool_hbm,
    out_ref,
    x_ref, qw_ref, kvw_ref, ow_ref, pool_ref, place_ref, load_sem, xs, outp, kv, fresh, qacc, kvacc, qt, acc, top, tot, thr_ref, cos_ref, sin_ref, part, mine, pairin, bsum, landed, relay,
    x_send, x_recv, xf_send, xf_recv, p_send, p_recv, pf_send, pf_recv,
    n_send, n_recv, nf_send, nf_recv, r_send, r_recv, s_send, s_recv,
):
    group = lax.axis_index("group")
    seq = lax.axis_index("seq")
    tensor = lax.axis_index("tensor")
    chip = tensor // 2
    core = tensor % 2
    gy = group // 4
    gz = group % 4
    partner = {"tensor": chip * 2 + (1 - core)}

    def chip_at(d):
        return {"tensor": ((chip + d) % 4) * 2 + core}

    def group_to(s):
        dy, dz = s // 4, s % 4
        return ((gy + dy) % 4) * 4 + (gz + dz) % 4

    def group_from(s):
        dy, dz = s // 4, s % 4
        return ((gy - dy + 4) % 4) * 4 + (gz - dz + 4) % 4

    def page_dev(s):
        if s % 4 == 2:
            return {"group": group_to(s), "seq": seq + 1 - 2 * (seq % 2)}
        return {"group": group_to(s)}

    def remote(src, dst, ss, rs, dev):
        return pltpu.make_async_remote_copy(
            src_ref=src, dst_ref=dst, send_sem=ss, recv_sem=rs, device_id=dev, device_id_type=MESH
        )

    barrier = pltpu.get_barrier_semaphore()
    for s in range(1, 16):
        pl.semaphore_signal(barrier, inc=1, device_id=page_dev(s), device_id_type=MESH)
    for b in range(1, 4):
        pl.semaphore_signal(barrier, inc=1, device_id={"seq": (seq + b) % 4}, device_id_type=MESH)
    for d in range(1, 4):
        if d != 2:
            pl.semaphore_signal(barrier, inc=1, device_id=chip_at(d), device_id_type=MESH)
    pl.semaphore_signal(barrier, inc=1, device_id=partner, device_id_type=MESH)

    loads = [
        pltpu.make_async_copy(src, dst, load_sem.at[i])
        for i, (src, dst) in enumerate(
            [(pool_hbm, pool_ref), (x_hbm, x_ref), (qw_hbm, qw_ref), (kvw_hbm, kvw_ref), (ow_hbm, ow_ref)]
        )
    ]
    for copy in loads:
        copy.start()

    mine_req = slots_ref[group]
    length = lengths_ref[mine_req]
    loads[0].wait()

    def pick(s, carry):
        req = slots_ref[group_to(s)]
        at = 0
        for w in range(16):
            off = table_ref[req, w] - group * 16
            at = at + jnp.where((off >= 0) & (off < 16), off, 0)
        outp[s] = pool_ref[at]
        return carry

    lax.fori_loop(0, 16, pick, 0)
    kv[core, 0] = outp[0]
    loads[1].wait()
    pl.semaphore_wait(barrier, 21)

    first = {d: remote(x_ref, xs.at[0, 4 - d], x_send.at[d], x_recv.at[4 - d], chip_at(d)) for d in (1, 3)}
    own_x = remote(x_ref, xs.at[1, 0], xf_send.at[0], xf_recv.at[0], partner)
    for d in (1, 3):
        first[d].start()
    own_x.start()
    order = [1, 3, 4, 8, 12, 5, 7, 9, 11, 13, 15, 2, 6, 10, 14]
    pages = {
        s: remote(outp.at[s], kv.at[core, s], p_send.at[s], p_recv.at[s], page_dev(s)) for s in order
    }
    for s in (2, 6, 10, 14, 1, 3, 5, 7, 9, 11, 13, 15, 4, 8, 12):
        pages[s].start()
    pagef = {
        s: remote(kv.at[core, s], kv.at[core, s], pf_send.at[s], pf_recv.at[s], partner) for s in range(16)
    }
    pagef[0].start()

    at_pos = lax.broadcasted_iota(jnp.int32, (32, 256), 1) + (length + seq * 256)
    angles = at_pos.astype(F32) * freq_ref[...]
    cos = jnp.cos(angles)
    sin = jnp.sin(angles)
    cos_ref[...] = cos
    sin_ref[...] = sin
    thr_ref[...] = jnp.maximum(
        lax.broadcasted_iota(jnp.int32, (1, 256), 1) + seq * 256, WINDOW - 1 - length
    )
    for h in range(4):
        acc[h] = jnp.zeros((HD, 256), F32)
        top[h] = jnp.full((1, 256), FLOOR, F32)
        tot[h] = jnp.zeros((1, 256), F32)

    my_ids = [table_ref[mine_req, w] for w in range(16)]

    def find_place(s, carry):
        low = group_from(s) * 16
        at = 0
        for w in range(16):
            off = my_ids[w] - low
            at = at + jnp.where((off >= 0) & (off < 16), w, 0)
        place_ref[s] = at
        return carry

    lax.fori_loop(0, 16, find_place, 0)

    loads[2].wait()
    loads[3].wait()

    def project(p, d):
        block = x_ref[...] if (p, d) == (0, 0) else xs[p, d]
        t = ((chip + d) % 4) * 2 + (core if p == 0 else 1 - core)
        rows = pl.ds(pl.multiple_of(t * 256, 256), 256)
        q = jnp.dot(block, qw_ref[rows, :], preferred_element_type=F32)
        f = lax.dot_general(kvw_ref[:, rows], block, (((1,), (1,)), ((), ())), preferred_element_type=F32)
        if (p, d) == (0, 0):
            qacc[...] = q
            kvacc[...] = f
        else:
            qacc[...] += q
            kvacc[...] += f

    project(0, 0)
    xf = {d: remote(xs.at[0, d], xs.at[1, d], xf_send.at[d], xf_recv.at[d], partner) for d in (1, 2, 3)}
    from_slot = 3 - 2 * core
    on = {"tensor": ((chip + 1 + 2 * core) % 4) * 2 + core}
    first[3].wait_recv()
    first[1].wait_recv()
    second = remote(xs.at[0, from_slot], xs.at[0, 2], x_send.at[2], x_recv.at[2], on)
    second.start()
    xf[1].start()
    xf[3].start()
    own_x.wait_recv()
    project(1, 0)
    project(0, 1)
    project(0, 3)
    xf[1].wait_recv()
    project(1, 1)
    xf[3].wait_recv()
    project(1, 3)
    second.wait_recv()
    xf[2].start()
    project(0, 2)
    xf[2].wait_recv()
    project(1, 2)

    is_key = jnp.where(core == 0, 1.0, 0.0).astype(F32)
    cos = cos_ref[...]
    sin = sin_ref[...]
    kcos = cos * is_key + (1.0 - is_key)
    ksin = sin * is_key
    a = kvacc[:32, :]
    b = kvacc[32:, :]
    fresh[core, 0] = jnp.concatenate([a * kcos - b * ksin, b * kcos + a * ksin], axis=0).astype(BF16)
    for step in range(1, 4):
        @pl.when(seq + step < 4)
        def _():
            remote(
                fresh.at[core, 0], fresh.at[core, step], n_send.at[step], n_recv.at[step], {"seq": (seq + step) % 4}
            ).start()
    newf = {
        i: remote(fresh.at[core, i], fresh.at[core, i], nf_send.at[i], nf_recv.at[i], partner) for i in range(4)
    }
    newf[0].start()
    for h in range(4):
        w = qacc[:, h * HD:(h + 1) * HD].T
        a = w[:32, :] * 0.125
        b = w[32:, :] * 0.125
        qt[h] = jnp.concatenate([a * cos - b * sin, b * cos + a * sin], axis=0).astype(BF16)

    def fold(keys, values, mask):
        kb = keys.T

        def head_pair(i, carry):
            scores = [jnp.dot(kb, qt[2 * i + k], preferred_element_type=F32) for k in range(2)]
            for k in range(2):
                h = 2 * i + k
                s = mask(scores[k])
                old = top[h]
                new = jnp.maximum(old, jnp.max(s, axis=0, keepdims=True))
                p = jnp.exp(s - new)
                alpha = jnp.exp(old - new)
                top[h] = new
                tot[h] = tot[h] * alpha + jnp.sum(p, axis=0, keepdims=True)
                acc[h] = acc[h] * alpha + jnp.dot(values, p.astype(BF16), preferred_element_type=F32)
            return carry

        lax.fori_loop(0, 2, head_pair, 0)

    row = lax.broadcasted_iota(jnp.int32, (PAGE, 256), 0)

    def fold_pages(slots):
        def mask(s):
            pieces = []
            for i, slot in enumerate(slots):
                low = thr_ref[...] - place_ref[slot] * PAGE
                pieces.append(jnp.where(row > low, s[i * PAGE:(i + 1) * PAGE], NEG))
            return jnp.concatenate(pieces, axis=0)

        fold(
            jnp.concatenate([kv[0, s] for s in slots], axis=1),
            jnp.concatenate([kv[1, s] for s in slots], axis=1),
            mask,
        )

    def take(slots):
        for s in slots:
            pages[s].wait_recv()
            pagef[s].start()

    def ready(slots):
        for s in slots:
            remote(kv.at[core, s], kv.at[1 - core, s], pf_send.at[s], pf_recv.at[s], partner).wait_recv()

    causal = lax.broadcasted_iota(jnp.int32, (256, 256), 0) <= lax.broadcasted_iota(jnp.int32, (256, 256), 1)

    def new_ready(i):
        remote(fresh.at[core, i], fresh.at[1 - core, i], nf_send.at[i], nf_recv.at[i], partner).wait_recv()

    new_ready(0)
    fold(fresh[0, 0], fresh[1, 0], lambda s: jnp.where(causal, s, NEG))
    c0, c1, c2, c3 = [0, 4, 8, 12], [1, 3, 5, 7], [9, 11, 13, 15], [2, 6, 10, 14]
    take(c0[1:])
    take(c1)
    ready(c0)
    fold_pages(c0)
    take(c2)
    ready(c1)
    fold_pages(c1)
    take(c3)
    ready(c2)
    fold_pages(c2)
    for step in range(1, 4):
        @pl.when(seq >= step)
        def _():
            remote(
                fresh.at[core, 0], fresh.at[core, step], n_send.at[step], n_recv.at[step], {"seq": (seq + step) % 4}
            ).wait_recv()
            newf[step].start()
    ready(c3)
    fold_pages(c3)
    for step in range(1, 4):
        @pl.when(seq >= step)
        def _():
            new_ready(step)
            fold(fresh[0, step], fresh[1, step], lambda s: s)

    loads[4].wait()
    heads = jnp.concatenate([(acc[h] / tot[h]).T.astype(BF16) for h in range(4)], axis=1)

    def partial_for(d, c):
        cols = pl.ds(pl.multiple_of((((chip + d) % 4) * 2 + c) * 256, 256), 256)
        return jnp.dot(heads, ow_ref[:, cols], preferred_element_type=F32).astype(BF16)

    near = 1 + 2 * core
    far = 3 - 2 * core
    up = {"tensor": ((chip + near) % 4) * 2 + core}
    down = {"tensor": ((chip + far) % 4) * 2 + core}
    halves = [pl.ds(0, 128), pl.ds(128, 128)]
    rs = {}
    for d in (2, 1, 3, 0):
        part[d] = partial_for(d, 1 - core)
        rs[d] = remote(part.at[d], pairin.at[d], r_send.at[d], r_recv.at[d], partner)
        rs[d].start()
        if d == 2:
            mine[2] = partial_for(2, core)
    rs[2].wait_recv()
    s2, s1 = [], []
    for i, half in enumerate(halves):
        bsum[0, half] = (mine[2, half].astype(F32) + pairin[2, half].astype(F32)).astype(BF16)
        s2.append(remote(bsum.at[0, half], landed.at[0, half], s_send.at[i], s_recv.at[i], up))
        s2[i].start()
    mine[1] = partial_for(1, core)
    mine[3] = partial_for(3, core)
    rs[1].wait_recv()
    rs[3].wait_recv()
    bsum[1] = (mine[far].astype(F32) + pairin[far].astype(F32)).astype(BF16)
    s3 = remote(bsum.at[1], landed.at[1], s_send.at[2], s_recv.at[2], down)
    s3.start()
    mine[0] = partial_for(0, core)
    for i, half in enumerate(halves):
        nearsum = mine[near, half].astype(F32) + pairin[near, half].astype(F32)
        s2[i].wait_recv()
        relay[half] = (nearsum + landed[0, half].astype(F32)).astype(BF16)
        s1.append(remote(relay.at[half], landed.at[2, half], s_send.at[3 + i], s_recv.at[3 + i], up))
        s1[i].start()
    rs[0].wait_recv()
    s3.wait_recv()
    for i, half in enumerate(halves):
        total = mine[0, half].astype(F32) + pairin[0, half].astype(F32) + landed[1, half].astype(F32)
        s1[i].wait_recv()
        out_ref[half] = (total + landed[2, half].astype(F32)).astype(BF16)

    for copy in [first[1], first[3], own_x, second, xf[1], xf[2], xf[3], *s1, *s2, s3]:
        copy.wait_send()
    for s in range(1, 16):
        pages[s].wait_send()
    for s in range(16):
        pagef[s].wait_send()
    for d in range(4):
        rs[d].wait_send()
    newf[0].wait_send()
    for step in range(1, 4):
        @pl.when(seq >= step)
        def _():
            newf[step].wait_send()

        @pl.when(seq + step < 4)
        def _():
            remote(
                fresh.at[core, 0], fresh.at[core, step], n_send.at[step], n_recv.at[step], {"seq": (seq + step) % 4}
            ).wait_send()


def shards(
    span_tokens, q_weight, kv_weight, out_weight, kv_pool, cache_lengths, slot_requests, page_table
):
    half_dim = HD // 2
    frequency = np.power(10000.0, -np.arange(half_dim) / half_dim).astype(np.float32)
    frequency = jnp.asarray(np.repeat(frequency[:, None], 256, axis=1))
    smem = pl.BlockSpec(memory_space=pltpu.SMEM)
    vmem = pl.BlockSpec(memory_space=pltpu.VMEM)
    hbm = pl.BlockSpec(memory_space=pl.ANY)
    dma = pltpu.SemaphoreType.DMA
    out = pl.pallas_call(
        layer_kernel,
        out_shape=jax.ShapeDtypeStruct((256, 256), BF16),
        in_specs=[smem] * 3 + [vmem] + [hbm] * 5,
        out_specs=vmem,
        scratch_shapes=[
            pltpu.VMEM((256, 256), BF16),
            pltpu.VMEM((2048, 256), BF16),
            pltpu.VMEM((HD, 2048), BF16),
            pltpu.VMEM((256, 2048), BF16),
            pltpu.VMEM((16, HD, PAGE), BF16),
            pltpu.SMEM((16,), jnp.int32),
            dma((5,)),
            pltpu.VMEM((2, 4, 256, 256), BF16),
            pltpu.VMEM((16, HD, PAGE), BF16),
            pltpu.VMEM((2, 16, HD, PAGE), BF16),
            pltpu.VMEM((2, 4, HD, 256), BF16),
            pltpu.VMEM((256, 256), F32),
            pltpu.VMEM((HD, 256), F32),
            pltpu.VMEM((4, HD, 256), BF16),
            pltpu.VMEM((4, HD, 256), F32),
            pltpu.VMEM((4, 1, 256), F32),
            pltpu.VMEM((4, 1, 256), F32),
            pltpu.VMEM((1, 256), jnp.int32),
            pltpu.VMEM((32, 256), F32),
            pltpu.VMEM((32, 256), F32),
            pltpu.VMEM((4, 256, 256), BF16),
            pltpu.VMEM((4, 256, 256), BF16),
            pltpu.VMEM((4, 256, 256), BF16),
            pltpu.VMEM((2, 256, 256), BF16),
            pltpu.VMEM((3, 256, 256), BF16),
            pltpu.VMEM((256, 256), BF16),
            dma((4,)), dma((4,)), dma((4,)), dma((4,)),
            dma((16,)), dma((16,)), dma((16,)), dma((16,)),
            dma((4,)), dma((4,)), dma((4,)), dma((4,)),
            dma((4,)), dma((4,)), dma((5,)), dma((5,)),
        ],
        compiler_params=pltpu.CompilerParams(
            collective_id=0, has_side_effects=True, vmem_limit_bytes=63 * 1024 * 1024
        ),
    )(
        slot_requests, cache_lengths, page_table, frequency,
        span_tokens.reshape(256, 256), q_weight, kv_weight.T, out_weight, jnp.swapaxes(kv_pool, 1, 2),
    )
    return out.reshape(1, 256, 256)


def solution(mesh):
    placed = (
        P("group", "seq", "tensor"),
        P(None, "tensor"),
        P(None, "tensor"),
        P("tensor", None),
        P("group", None, "tensor"),
        P(),
        P(),
        P(),
    )
    return jax.shard_map(
        shards, mesh=mesh, in_specs=placed, out_specs=P("group", "seq", "tensor"), check_vma=False
    )
```

```python
import jax
import jax.numpy as jnp
import numpy as np
from jax import lax
from jax.experimental import pallas as pl
from jax.experimental.pallas import tpu as pltpu
from jax.sharding import PartitionSpec as P

HD = 64
WINDOW = 2048
PAGE = 128
MESH = pl.DeviceIdType.MESH
NEG = -1e30
FLOOR = -1e20
F32 = jnp.float32
BF16 = jnp.bfloat16


def layer_kernel(
    slots_ref, lengths_ref, table_ref, freq_hbm, x_hbm, qw_hbm, kvw_hbm, ow_hbm, pool_hbm,
    out_ref,
    x_ref, qw_ref, kvw_ref, ow_ref, pool_ref, freq_ref, place_ref, load_sem, xs, outp, kv, fresh, qacc, kvacc, qt, acc, top, tot, thr_ref, cos_ref, sin_ref, part, mine, pairin, bsum, landed, relay,
    x_send, x_recv, xf_send, xf_recv, p_send, p_recv, pf_send, pf_recv,
    n_send, n_recv, nf_send, nf_recv, r_send, r_recv, s_send, s_recv,
):
    group = lax.axis_index("group")
    seq = lax.axis_index("seq")
    tensor = lax.axis_index("tensor")
    chip = tensor // 2
    core = tensor % 2
    gy = group // 4
    gz = group % 4
    partner = {"tensor": chip * 2 + (1 - core)}

    def chip_at(d):
        return {"tensor": ((chip + d) % 4) * 2 + core}

    def group_to(s):
        dy, dz = s // 4, s % 4
        return ((gy + dy) % 4) * 4 + (gz + dz) % 4

    def group_from(s):
        dy, dz = s // 4, s % 4
        return ((gy - dy + 4) % 4) * 4 + (gz - dz + 4) % 4

    def page_dev(s):
        if s % 4 == 2:
            return {"group": group_to(s), "seq": seq + 1 - 2 * (seq % 2)}
        return {"group": group_to(s)}

    def remote(src, dst, ss, rs, dev):
        return pltpu.make_async_remote_copy(
            src_ref=src, dst_ref=dst, send_sem=ss, recv_sem=rs, device_id=dev, device_id_type=MESH
        )

    barrier = pltpu.get_barrier_semaphore()
    for s in range(1, 16):
        pl.semaphore_signal(barrier, inc=1, device_id=page_dev(s), device_id_type=MESH)
    for b in range(1, 4):
        pl.semaphore_signal(barrier, inc=1, device_id={"seq": (seq + b) % 4}, device_id_type=MESH)
    for d in range(1, 4):
        if d != 2:
            pl.semaphore_signal(barrier, inc=1, device_id=chip_at(d), device_id_type=MESH)
    pl.semaphore_signal(barrier, inc=1, device_id=partner, device_id_type=MESH)

    loads = [
        pltpu.make_async_copy(src, dst, load_sem.at[i])
        for i, (src, dst) in enumerate(
            [(pool_hbm, pool_ref), (x_hbm, x_ref), (qw_hbm, qw_ref), (kvw_hbm, kvw_ref), (ow_hbm, ow_ref), (freq_hbm, freq_ref)]
        )
    ]
    for copy in loads:
        copy.start()

    mine_req = slots_ref[group]
    length = lengths_ref[mine_req]
    loads[0].wait()

    def pick(s, carry):
        req = slots_ref[group_to(s)]
        at = 0
        for w in range(16):
            off = table_ref[req, w] - group * 16
            at = at + jnp.where((off & -16) == 0, off, 0)
        outp[s] = pool_ref[at]
        return carry

    lax.fori_loop(0, 16, pick, 0)
    kv[core, 0] = outp[0]
    loads[1].wait()
    pl.semaphore_wait(barrier, 21)

    fwd = 1 + 2 * core
    back = 3 - 2 * core
    halves = [pl.ds(0, 128), pl.ds(128, 128)]
    first = [
        remote(x_ref.at[half], xs.at[0, back, half], x_send.at[i], x_recv.at[i], chip_at(fwd))
        for i, half in enumerate(halves)
    ]
    first.append(remote(x_ref, xs.at[0, fwd], x_send.at[2], x_recv.at[2], chip_at(back)))
    own_x = remote(x_ref, xs.at[1, 0], xf_send.at[0], xf_recv.at[0], partner)
    for copy in first:
        copy.start()
    own_x.start()
    order = [1, 3, 4, 8, 12, 5, 7, 9, 11, 13, 15, 2, 6, 10, 14]
    pages = {
        s: remote(outp.at[s], kv.at[core, s], p_send.at[s], p_recv.at[s], page_dev(s)) for s in order
    }
    for s in (2, 6, 10, 14, 1, 3, 5, 7, 9, 11, 13, 15, 4, 8, 12):
        pages[s].start()
    pagef = {
        s: remote(kv.at[core, s], kv.at[core, s], pf_send.at[s], pf_recv.at[s], partner) for s in range(16)
    }
    pagef[0].start()

    loads[5].wait()
    at_pos = lax.broadcasted_iota(jnp.int32, (32, 256), 1) + (length + seq * 256)
    angles = at_pos.astype(F32) * freq_ref[...]
    cos = jnp.cos(angles)
    sin = jnp.sin(angles)
    cos_ref[...] = cos
    sin_ref[...] = sin
    thr_ref[...] = jnp.maximum(
        lax.broadcasted_iota(jnp.int32, (1, 256), 1) + seq * 256, WINDOW - 1 - length
    )
    for h in range(4):
        acc[h] = jnp.zeros((HD, 256), F32)
        top[h] = jnp.full((1, 256), FLOOR, F32)
        tot[h] = jnp.zeros((1, 256), F32)

    my_ids = [table_ref[mine_req, w] for w in range(16)]

    def find_place(s, carry):
        low = group_from(s) * 16
        at = 0
        for w in range(16):
            off = my_ids[w] - low
            at = at + jnp.where((off & -16) == 0, w, 0)
        place_ref[s] = at
        return carry

    lax.fori_loop(0, 16, find_place, 0)

    loads[2].wait()
    loads[3].wait()

    def project(p, d, start=False):
        block = x_ref[...] if start else xs[p, d]
        t = ((chip + d) % 4) * 2 + (core if p == 0 else 1 - core)
        rows = pl.ds(pl.multiple_of(t * 256, 256), 256)
        q = jnp.dot(block, qw_ref[rows, :], preferred_element_type=F32)
        f = lax.dot_general(kvw_ref[:, rows], block, (((1,), (1,)), ((), ())), preferred_element_type=F32)
        if start:
            qacc[...] = q
            kvacc[...] = f
        else:
            qacc[...] += q
            kvacc[...] += f

    def hand_over(i, d):
        return remote(xs.at[0, d], xs.at[1, d], xf_send.at[i], xf_recv.at[i], partner)

    project(0, 0, True)
    second = []
    for i, half in enumerate(halves):
        first[i].wait_recv()
        second.append(
            remote(xs.at[0, back, half], xs.at[0, 2, half], x_send.at[3 + i], x_recv.at[3 + i], chip_at(fwd))
        )
        second[i].start()
    xf = [hand_over(1, back), hand_over(3, fwd), hand_over(2, 2)]
    xf[0].start()
    own_x.wait_recv()
    project(1, 0)
    project(0, back)
    first[2].wait_recv()
    xf[1].start()
    project(0, fwd)
    hand_over(1, fwd).wait_recv()
    project(1, fwd)
    hand_over(3, back).wait_recv()
    project(1, back)
    second[0].wait_recv()
    second[1].wait_recv()
    xf[2].start()
    project(0, 2)
    xf[2].wait_recv()
    project(1, 2)

    is_key = jnp.where(core == 0, 1.0, 0.0).astype(F32)
    cos = cos_ref[...]
    sin = sin_ref[...]
    kcos = cos * is_key + (1.0 - is_key)
    ksin = sin * is_key
    a = kvacc[:32, :]
    b = kvacc[32:, :]
    fresh[core, 0] = jnp.concatenate([a * kcos - b * ksin, b * kcos + a * ksin], axis=0).astype(BF16)
    for step in range(1, 4):
        @pl.when(seq + step < 4)
        def _():
            remote(
                fresh.at[core, 0], fresh.at[core, step], n_send.at[step], n_recv.at[step], {"seq": (seq + step) % 4}
            ).start()
    newf = {
        i: remote(fresh.at[core, i], fresh.at[core, i], nf_send.at[i], nf_recv.at[i], partner) for i in range(4)
    }
    newf[0].start()
    for h in range(4):
        w = qacc[:, h * HD:(h + 1) * HD].T
        a = w[:32, :] * 0.125
        b = w[32:, :] * 0.125
        qt[h] = jnp.concatenate([a * cos - b * sin, b * cos + a * sin], axis=0).astype(BF16)

    def fold(keys, values, mask):
        kb = keys.T

        def head_pair(i, carry):
            scores = [jnp.dot(kb, qt[2 * i + k], preferred_element_type=F32) for k in range(2)]
            for k in range(2):
                h = 2 * i + k
                s = mask(scores[k])
                old = top[h]
                new = jnp.maximum(old, jnp.max(s, axis=0, keepdims=True))
                p = jnp.exp(s - new)
                alpha = jnp.exp(old - new)
                top[h] = new
                tot[h] = tot[h] * alpha + jnp.sum(p, axis=0, keepdims=True)
                acc[h] = acc[h] * alpha + jnp.dot(values, p.astype(BF16), preferred_element_type=F32)
            return carry

        lax.fori_loop(0, 2, head_pair, 0)

    row = lax.broadcasted_iota(jnp.int32, (PAGE, 256), 0)

    def fold_pages(slots):
        def mask(s):
            pieces = []
            for i, slot in enumerate(slots):
                low = thr_ref[...] - place_ref[slot] * PAGE
                pieces.append(jnp.where(row > low, s[i * PAGE:(i + 1) * PAGE], NEG))
            return jnp.concatenate(pieces, axis=0)

        fold(
            jnp.concatenate([kv[0, s] for s in slots], axis=1),
            jnp.concatenate([kv[1, s] for s in slots], axis=1),
            mask,
        )

    def take(slots):
        for s in slots:
            pages[s].wait_recv()
            pagef[s].start()

    def ready(slots):
        for s in slots:
            remote(kv.at[core, s], kv.at[1 - core, s], pf_send.at[s], pf_recv.at[s], partner).wait_recv()

    causal = lax.broadcasted_iota(jnp.int32, (256, 256), 0) <= lax.broadcasted_iota(jnp.int32, (256, 256), 1)

    def new_ready(i):
        remote(fresh.at[core, i], fresh.at[1 - core, i], nf_send.at[i], nf_recv.at[i], partner).wait_recv()

    take([4, 8, 12])
    new_ready(0)
    fold(fresh[0, 0], fresh[1, 0], lambda s: jnp.where(causal, s, NEG))
    c0, c1, c2, c3 = [0, 4, 8, 12], [1, 3, 5, 7], [9, 11, 13, 15], [2, 6, 10, 14]
    ready(c0)
    fold_pages(c0)
    take(c1)
    take(c2)
    ready(c1)
    fold_pages(c1)
    take(c3)
    ready(c2)
    fold_pages(c2)
    for step in range(1, 4):
        @pl.when(seq >= step)
        def _():
            remote(
                fresh.at[core, 0], fresh.at[core, step], n_send.at[step], n_recv.at[step], {"seq": (seq + step) % 4}
            ).wait_recv()
            newf[step].start()
    ready(c3)
    fold_pages(c3)
    for step in range(1, 4):
        @pl.when(seq >= step)
        def _():
            new_ready(step)
            fold(fresh[0, step], fresh[1, step], lambda s: s)

    loads[4].wait()
    heads = jnp.concatenate([(acc[h] / tot[h]).T.astype(BF16) for h in range(4)], axis=1)

    def partial_for(d, c):
        cols = pl.ds(pl.multiple_of((((chip + d) % 4) * 2 + c) * 256, 256), 256)
        return jnp.dot(heads, ow_ref[:, cols], preferred_element_type=F32).astype(BF16)

    near = 1 + 2 * core
    far = 3 - 2 * core
    up = {"tensor": ((chip + near) % 4) * 2 + core}
    down = {"tensor": ((chip + far) % 4) * 2 + core}
    rs = {}
    for d in (2, 1, 3, 0):
        part[d] = partial_for(d, 1 - core)
        rs[d] = remote(part.at[d], pairin.at[d], r_send.at[d], r_recv.at[d], partner)
        rs[d].start()
        if d == 2:
            mine[2] = partial_for(2, core)
    rs[2].wait_recv()
    s2, s1 = [], []
    for i, half in enumerate(halves):
        bsum[0, half] = (mine[2, half].astype(F32) + pairin[2, half].astype(F32)).astype(BF16)
        s2.append(remote(bsum.at[0, half], landed.at[0, half], s_send.at[i], s_recv.at[i], up))
        s2[i].start()
    mine[1] = partial_for(1, core)
    mine[3] = partial_for(3, core)
    rs[1].wait_recv()
    rs[3].wait_recv()
    bsum[1] = (mine[far].astype(F32) + pairin[far].astype(F32)).astype(BF16)
    s3 = remote(bsum.at[1], landed.at[1], s_send.at[2], s_recv.at[2], down)
    s3.start()
    mine[0] = partial_for(0, core)
    for i, half in enumerate(halves):
        nearsum = mine[near, half].astype(F32) + pairin[near, half].astype(F32)
        s2[i].wait_recv()
        relay[half] = (nearsum + landed[0, half].astype(F32)).astype(BF16)
        s1.append(remote(relay.at[half], landed.at[2, half], s_send.at[3 + i], s_recv.at[3 + i], up))
        s1[i].start()
    rs[0].wait_recv()
    s3.wait_recv()
    for i, half in enumerate(halves):
        total = mine[0, half].astype(F32) + pairin[0, half].astype(F32) + landed[1, half].astype(F32)
        s1[i].wait_recv()
        out_ref[half] = (total + landed[2, half].astype(F32)).astype(BF16)

    for copy in [*first, own_x, *second, *xf, *s1, *s2, s3]:
        copy.wait_send()
    for s in range(1, 16):
        pages[s].wait_send()
    for s in range(16):
        pagef[s].wait_send()
    for d in range(4):
        rs[d].wait_send()
    newf[0].wait_send()
    for step in range(1, 4):
        @pl.when(seq >= step)
        def _():
            newf[step].wait_send()

        @pl.when(seq + step < 4)
        def _():
            remote(
                fresh.at[core, 0], fresh.at[core, step], n_send.at[step], n_recv.at[step], {"seq": (seq + step) % 4}
            ).wait_send()


def shards(
    span_tokens, q_weight, kv_weight, out_weight, kv_pool, cache_lengths, slot_requests, page_table
):
    half_dim = HD // 2
    frequency = np.power(10000.0, -np.arange(half_dim) / half_dim).astype(np.float32)
    frequency = jnp.asarray(np.repeat(frequency[:, None], 256, axis=1))
    smem = pl.BlockSpec(memory_space=pltpu.SMEM)
    vmem = pl.BlockSpec(memory_space=pltpu.VMEM)
    hbm = pl.BlockSpec(memory_space=pl.ANY)
    dma = pltpu.SemaphoreType.DMA
    out = pl.pallas_call(
        layer_kernel,
        out_shape=jax.ShapeDtypeStruct((256, 256), BF16),
        in_specs=[smem] * 3 + [hbm] * 6,
        out_specs=vmem,
        scratch_shapes=[
            pltpu.VMEM((256, 256), BF16),
            pltpu.VMEM((2048, 256), BF16),
            pltpu.VMEM((HD, 2048), BF16),
            pltpu.VMEM((256, 2048), BF16),
            pltpu.VMEM((16, HD, PAGE), BF16),
            pltpu.VMEM((32, 256), F32),
            pltpu.SMEM((16,), jnp.int32),
            dma((6,)),
            pltpu.VMEM((2, 4, 256, 256), BF16),
            pltpu.VMEM((16, HD, PAGE), BF16),
            pltpu.VMEM((2, 16, HD, PAGE), BF16),
            pltpu.VMEM((2, 4, HD, 256), BF16),
            pltpu.VMEM((256, 256), F32),
            pltpu.VMEM((HD, 256), F32),
            pltpu.VMEM((4, HD, 256), BF16),
            pltpu.VMEM((4, HD, 256), F32),
            pltpu.VMEM((4, 1, 256), F32),
            pltpu.VMEM((4, 1, 256), F32),
            pltpu.VMEM((1, 256), jnp.int32),
            pltpu.VMEM((32, 256), F32),
            pltpu.VMEM((32, 256), F32),
            pltpu.VMEM((4, 256, 256), BF16),
            pltpu.VMEM((4, 256, 256), BF16),
            pltpu.VMEM((4, 256, 256), BF16),
            pltpu.VMEM((2, 256, 256), BF16),
            pltpu.VMEM((3, 256, 256), BF16),
            pltpu.VMEM((256, 256), BF16),
            dma((5,)), dma((5,)), dma((4,)), dma((4,)),
            dma((16,)), dma((16,)), dma((16,)), dma((16,)),
            dma((4,)), dma((4,)), dma((4,)), dma((4,)),
            dma((4,)), dma((4,)), dma((5,)), dma((5,)),
        ],
        compiler_params=pltpu.CompilerParams(
            collective_id=0, has_side_effects=True, vmem_limit_bytes=63 * 1024 * 1024
        ),
    )(
        slot_requests, cache_lengths, page_table, frequency,
        span_tokens.reshape(256, 256), q_weight, kv_weight.T, out_weight, jnp.swapaxes(kv_pool, 1, 2),
    )
    return out.reshape(1, 256, 256)


def solution(mesh):
    placed = (
        P("group", "seq", "tensor"),
        P(None, "tensor"),
        P(None, "tensor"),
        P("tensor", None),
        P("group", None, "tensor"),
        P(),
        P(),
        P(),
    )
    return jax.shard_map(
        shards, mesh=mesh, in_specs=placed, out_specs=P("group", "seq", "tensor"), check_vma=False
    )
```

```python
import jax
import jax.numpy as jnp
import numpy as np
from jax import lax
from jax.experimental import pallas as pl
from jax.experimental.pallas import tpu as pltpu
from jax.sharding import PartitionSpec as P

HD = 64
WINDOW = 2048
PAGE = 128
MESH = pl.DeviceIdType.MESH
NEG = -1e30
FLOOR = -1e20
F32 = jnp.float32
BF16 = jnp.bfloat16


def layer_kernel(
    slots_ref, lengths_ref, table_ref, freq_hbm, x_hbm, qw_hbm, kvw_hbm, ow_hbm, pool_hbm,
    out_ref,
    x_ref, qw_ref, kvw_ref, ow_ref, pool_ref, freq_ref, place_ref, load_sem, xs, outp, kv, fresh, qacc, kvacc, qt, acc, top, tot, thr_ref, cos_ref, sin_ref, part, mine, pairin, bsum, landed, relay,
    x_send, x_recv, xf_send, xf_recv, p_send, p_recv, z_send, z_recv, pf_send, pf_recv,
    n_send, n_recv, nf_send, nf_recv, r_send, r_recv, s_send, s_recv,
):
    group = lax.axis_index("group")
    seq = lax.axis_index("seq")
    tensor = lax.axis_index("tensor")
    chip = tensor // 2
    core = tensor % 2
    gy = group // 4
    gz = group % 4
    partner = {"tensor": chip * 2 + (1 - core)}

    def chip_at(d):
        return {"tensor": ((chip + d) % 4) * 2 + core}

    def group_to(s):
        dy, dz = s // 4, s % 4
        return ((gy + dy) % 4) * 4 + (gz + dz) % 4

    def group_from(s):
        dy, dz = s // 4, s % 4
        return ((gy - dy + 4) % 4) * 4 + (gz - dz + 4) % 4

    def page_dev(s):
        if s % 4 == 2:
            return {"group": group_to(s), "seq": seq + 1 - 2 * (seq % 2)}
        return {"group": group_to(s)}

    def remote(src, dst, ss, rs, dev):
        return pltpu.make_async_remote_copy(
            src_ref=src, dst_ref=dst, send_sem=ss, recv_sem=rs, device_id=dev, device_id_type=MESH
        )

    barrier = pltpu.get_barrier_semaphore()
    for s in range(1, 16):
        pl.semaphore_signal(barrier, inc=1, device_id=page_dev(s), device_id_type=MESH)
    for b in range(1, 4):
        pl.semaphore_signal(barrier, inc=1, device_id={"seq": (seq + b) % 4}, device_id_type=MESH)
    for d in range(1, 4):
        if d != 2:
            pl.semaphore_signal(barrier, inc=1, device_id=chip_at(d), device_id_type=MESH)
    pl.semaphore_signal(barrier, inc=1, device_id=partner, device_id_type=MESH)

    loads = [
        pltpu.make_async_copy(src, dst, load_sem.at[i])
        for i, (src, dst) in enumerate(
            [(pool_hbm, pool_ref), (x_hbm, x_ref), (qw_hbm, qw_ref), (kvw_hbm, kvw_ref), (ow_hbm, ow_ref), (freq_hbm, freq_ref)]
        )
    ]
    for copy in loads:
        copy.start()

    mine_req = slots_ref[group]
    length = lengths_ref[mine_req]
    loads[0].wait()

    def pick(s, carry):
        req = slots_ref[group_to(s)]
        at = 0
        for w in range(16):
            off = table_ref[req, w] - group * 16
            at = at + jnp.where((off & -16) == 0, off, 0)
        outp[s] = pool_ref[at]
        return carry

    lax.fori_loop(0, 16, pick, 0)
    kv[core, 0] = outp[0]
    loads[1].wait()
    pl.semaphore_wait(barrier, 21)

    fwd = 1 + 2 * core
    back = 3 - 2 * core
    halves = [pl.ds(0, 128), pl.ds(128, 128)]
    first = [
        remote(x_ref.at[half], xs.at[0, back, half], x_send.at[i], x_recv.at[i], chip_at(fwd))
        for i, half in enumerate(halves)
    ]
    first.append(remote(x_ref, xs.at[0, fwd], x_send.at[2], x_recv.at[2], chip_at(back)))
    own_x = remote(x_ref, xs.at[1, 0], xf_send.at[0], xf_recv.at[0], partner)
    for copy in first:
        copy.start()
    own_x.start()
    odd = seq % 2
    near_seq = {"seq": seq + 1 - 2 * odd}

    def page_copy(s, dev):
        return remote(outp.at[s], kv.at[core, s], p_send.at[s], p_recv.at[s], dev)

    def far_slots(parity, dzs):
        return [(2 * k + parity) * 4 + dz for dz in dzs for k in range(2)]

    sent = [
        page_copy(s, {"group": group_to(s), "seq": seq + 1 - 2 * odd}) for s in far_slots(1 - odd, [2])
    ]
    sent += [page_copy(s, {"group": group_to(s)}) for s in far_slots(odd, [1, 3]) + [4, 8, 12]]
    for copy in sent:
        copy.start()

    def page_pass(s):
        return remote(kv.at[core, s], kv.at[core, s], z_send.at[s], z_recv.at[s], near_seq)

    def page_share(s):
        return remote(kv.at[core, s], kv.at[core, s], pf_send.at[s], pf_recv.at[s], partner)

    page_share(0).start()

    loads[5].wait()
    at_pos = lax.broadcasted_iota(jnp.int32, (32, 256), 1) + (length + seq * 256)
    angles = at_pos.astype(F32) * freq_ref[...]
    cos = jnp.cos(angles)
    sin = jnp.sin(angles)
    cos_ref[...] = cos
    sin_ref[...] = sin
    thr_ref[...] = jnp.maximum(
        lax.broadcasted_iota(jnp.int32, (1, 256), 1) + seq * 256, WINDOW - 1 - length
    )
    for h in range(4):
        acc[h] = jnp.zeros((HD, 256), F32)
        top[h] = jnp.full((1, 256), FLOOR, F32)
        tot[h] = jnp.zeros((1, 256), F32)

    my_ids = [table_ref[mine_req, w] for w in range(16)]

    def find_place(s, carry):
        low = group_from(s) * 16
        at = 0
        for w in range(16):
            off = my_ids[w] - low
            at = at + jnp.where((off & -16) == 0, w, 0)
        place_ref[s] = at
        return carry

    lax.fori_loop(0, 16, find_place, 0)

    loads[2].wait()
    loads[3].wait()

    def project(p, d, start=False):
        block = x_ref[...] if start else xs[p, d]
        t = ((chip + d) % 4) * 2 + (core if p == 0 else 1 - core)
        rows = pl.ds(pl.multiple_of(t * 256, 256), 256)
        q = jnp.dot(block, qw_ref[rows, :], preferred_element_type=F32)
        f = lax.dot_general(kvw_ref[:, rows], block, (((1,), (1,)), ((), ())), preferred_element_type=F32)
        if start:
            qacc[...] = q
            kvacc[...] = f
        else:
            qacc[...] += q
            kvacc[...] += f

    def hand_over(i, d):
        return remote(xs.at[0, d], xs.at[1, d], xf_send.at[i], xf_recv.at[i], partner)

    project(0, 0, True)
    second = []
    for i, half in enumerate(halves):
        first[i].wait_recv()
        second.append(
            remote(xs.at[0, back, half], xs.at[0, 2, half], x_send.at[3 + i], x_recv.at[3 + i], chip_at(fwd))
        )
        second[i].start()
    xf = [hand_over(1, back), hand_over(3, fwd), hand_over(2, 2)]
    xf[0].start()
    own_x.wait_recv()
    project(1, 0)
    project(0, back)
    first[2].wait_recv()
    xf[1].start()
    project(0, fwd)
    hand_over(1, fwd).wait_recv()
    project(1, fwd)
    hand_over(3, back).wait_recv()
    project(1, back)
    second[0].wait_recv()
    second[1].wait_recv()
    xf[2].start()
    project(0, 2)
    xf[2].wait_recv()
    project(1, 2)

    is_key = jnp.where(core == 0, 1.0, 0.0).astype(F32)
    cos = cos_ref[...]
    sin = sin_ref[...]
    kcos = cos * is_key + (1.0 - is_key)
    ksin = sin * is_key
    a = kvacc[:32, :]
    b = kvacc[32:, :]
    fresh[core, 0] = jnp.concatenate([a * kcos - b * ksin, b * kcos + a * ksin], axis=0).astype(BF16)
    for step in range(1, 4):
        @pl.when(seq + step < 4)
        def _():
            remote(
                fresh.at[core, 0], fresh.at[core, step], n_send.at[step], n_recv.at[step], {"seq": (seq + step) % 4}
            ).start()
    newf = {
        i: remote(fresh.at[core, i], fresh.at[core, i], nf_send.at[i], nf_recv.at[i], partner) for i in range(4)
    }
    newf[0].start()
    for h in range(4):
        w = qacc[:, h * HD:(h + 1) * HD].T
        a = w[:32, :] * 0.125
        b = w[32:, :] * 0.125
        qt[h] = jnp.concatenate([a * cos - b * sin, b * cos + a * sin], axis=0).astype(BF16)

    def fold(keys, values, mask):
        kb = keys.T

        def head_pair(i, carry):
            scores = [jnp.dot(kb, qt[2 * i + k], preferred_element_type=F32) for k in range(2)]
            for k in range(2):
                h = 2 * i + k
                s = mask(scores[k])
                old = top[h]
                new = jnp.maximum(old, jnp.max(s, axis=0, keepdims=True))
                p = jnp.exp(s - new)
                alpha = jnp.exp(old - new)
                top[h] = new
                tot[h] = tot[h] * alpha + jnp.sum(p, axis=0, keepdims=True)
                acc[h] = acc[h] * alpha + jnp.dot(values, p.astype(BF16), preferred_element_type=F32)
            return carry

        lax.fori_loop(0, 2, head_pair, 0)

    row = lax.broadcasted_iota(jnp.int32, (PAGE, 256), 0)

    def fold_pages(slots):
        def mask(s):
            pieces = []
            for i, slot in enumerate(slots):
                low = thr_ref[...] - place_ref[slot] * PAGE
                pieces.append(jnp.where(row > low, s[i * PAGE:(i + 1) * PAGE], NEG))
            return jnp.concatenate(pieces, axis=0)

        fold(
            jnp.concatenate([kv[0, s] for s in slots], axis=1),
            jnp.concatenate([kv[1, s] for s in slots], axis=1),
            mask,
        )

    def take(slots, passed=False):
        for s in slots:
            page_copy(s, partner).wait_recv()
            if passed:
                page_pass(s).start()
            page_share(s).start()

    def take_passed(slots):
        for s in slots:
            page_pass(s).wait_recv()
            page_share(s).start()

    def ready(slots):
        for s in slots:
            remote(kv.at[core, s], kv.at[1 - core, s], pf_send.at[s], pf_recv.at[s], partner).wait_recv()

    causal = lax.broadcasted_iota(jnp.int32, (256, 256), 0) <= lax.broadcasted_iota(jnp.int32, (256, 256), 1)

    def new_ready(i):
        remote(fresh.at[core, i], fresh.at[1 - core, i], nf_send.at[i], nf_recv.at[i], partner).wait_recv()

    take([4, 8, 12])
    new_ready(0)
    fold(fresh[0, 0], fresh[1, 0], lambda s: jnp.where(causal, s, NEG))
    c0 = [0, 4, 8, 12]
    d1, d2 = far_slots(odd, [1, 3]), far_slots(odd, [2])
    e1, e2 = far_slots(1 - odd, [1, 3]), far_slots(1 - odd, [2])
    ready(c0)
    fold_pages(c0)
    take(d1, True)
    take(d2, True)
    ready(d1)
    fold_pages(d1)
    take_passed(e1)
    take_passed(e2)
    ready(e1)
    fold_pages(e1)
    for step in range(1, 4):
        @pl.when(seq >= step)
        def _():
            remote(
                fresh.at[core, 0], fresh.at[core, step], n_send.at[step], n_recv.at[step], {"seq": (seq + step) % 4}
            ).wait_recv()
            newf[step].start()
    ready(d2 + e2)
    fold_pages(d2 + e2)
    for step in range(1, 4):
        @pl.when(seq >= step)
        def _():
            new_ready(step)
            fold(fresh[0, step], fresh[1, step], lambda s: s)

    loads[4].wait()
    heads = jnp.concatenate([(acc[h] / tot[h]).T.astype(BF16) for h in range(4)], axis=1)

    def partial_for(d, c):
        cols = pl.ds(pl.multiple_of((((chip + d) % 4) * 2 + c) * 256, 256), 256)
        return jnp.dot(heads, ow_ref[:, cols], preferred_element_type=F32).astype(BF16)

    near = 1 + 2 * core
    far = 3 - 2 * core
    up = {"tensor": ((chip + near) % 4) * 2 + core}
    down = {"tensor": ((chip + far) % 4) * 2 + core}
    rs = {}
    for d in (2, 1, 3, 0):
        part[d] = partial_for(d, 1 - core)
        rs[d] = remote(part.at[d], pairin.at[d], r_send.at[d], r_recv.at[d], partner)
        rs[d].start()
        if d == 2:
            mine[2] = partial_for(2, core)
    rs[2].wait_recv()
    s2, s1 = [], []
    for i, half in enumerate(halves):
        bsum[0, half] = (mine[2, half].astype(F32) + pairin[2, half].astype(F32)).astype(BF16)
        s2.append(remote(bsum.at[0, half], landed.at[0, half], s_send.at[i], s_recv.at[i], up))
        s2[i].start()
    mine[1] = partial_for(1, core)
    mine[3] = partial_for(3, core)
    rs[1].wait_recv()
    rs[3].wait_recv()
    bsum[1] = (mine[far].astype(F32) + pairin[far].astype(F32)).astype(BF16)
    s3 = remote(bsum.at[1], landed.at[1], s_send.at[2], s_recv.at[2], down)
    s3.start()
    mine[0] = partial_for(0, core)
    for i, half in enumerate(halves):
        nearsum = mine[near, half].astype(F32) + pairin[near, half].astype(F32)
        s2[i].wait_recv()
        relay[half] = (nearsum + landed[0, half].astype(F32)).astype(BF16)
        s1.append(remote(relay.at[half], landed.at[2, half], s_send.at[3 + i], s_recv.at[3 + i], up))
        s1[i].start()
    rs[0].wait_recv()
    s3.wait_recv()
    for i, half in enumerate(halves):
        total = mine[0, half].astype(F32) + pairin[0, half].astype(F32) + landed[1, half].astype(F32)
        s1[i].wait_recv()
        out_ref[half] = (total + landed[2, half].astype(F32)).astype(BF16)

    for copy in [*first, own_x, *second, *xf, *s1, *s2, s3]:
        copy.wait_send()
    for copy in sent:
        copy.wait_send()
    for s in d1 + d2:
        page_pass(s).wait_send()
    for s in c0 + d1 + d2 + e1 + e2:
        page_share(s).wait_send()
    for d in range(4):
        rs[d].wait_send()
    newf[0].wait_send()
    for step in range(1, 4):
        @pl.when(seq >= step)
        def _():
            newf[step].wait_send()

        @pl.when(seq + step < 4)
        def _():
            remote(
                fresh.at[core, 0], fresh.at[core, step], n_send.at[step], n_recv.at[step], {"seq": (seq + step) % 4}
            ).wait_send()


def shards(
    span_tokens, q_weight, kv_weight, out_weight, kv_pool, cache_lengths, slot_requests, page_table
):
    half_dim = HD // 2
    frequency = np.power(10000.0, -np.arange(half_dim) / half_dim).astype(np.float32)
    frequency = jnp.asarray(np.repeat(frequency[:, None], 256, axis=1))
    smem = pl.BlockSpec(memory_space=pltpu.SMEM)
    vmem = pl.BlockSpec(memory_space=pltpu.VMEM)
    hbm = pl.BlockSpec(memory_space=pl.ANY)
    dma = pltpu.SemaphoreType.DMA
    out = pl.pallas_call(
        layer_kernel,
        out_shape=jax.ShapeDtypeStruct((256, 256), BF16),
        in_specs=[smem] * 3 + [hbm] * 6,
        out_specs=vmem,
        scratch_shapes=[
            pltpu.VMEM((256, 256), BF16),
            pltpu.VMEM((2048, 256), BF16),
            pltpu.VMEM((HD, 2048), BF16),
            pltpu.VMEM((256, 2048), BF16),
            pltpu.VMEM((16, HD, PAGE), BF16),
            pltpu.VMEM((32, 256), F32),
            pltpu.SMEM((16,), jnp.int32),
            dma((6,)),
            pltpu.VMEM((2, 4, 256, 256), BF16),
            pltpu.VMEM((16, HD, PAGE), BF16),
            pltpu.VMEM((2, 16, HD, PAGE), BF16),
            pltpu.VMEM((2, 4, HD, 256), BF16),
            pltpu.VMEM((256, 256), F32),
            pltpu.VMEM((HD, 256), F32),
            pltpu.VMEM((4, HD, 256), BF16),
            pltpu.VMEM((4, HD, 256), F32),
            pltpu.VMEM((4, 1, 256), F32),
            pltpu.VMEM((4, 1, 256), F32),
            pltpu.VMEM((1, 256), jnp.int32),
            pltpu.VMEM((32, 256), F32),
            pltpu.VMEM((32, 256), F32),
            pltpu.VMEM((4, 256, 256), BF16),
            pltpu.VMEM((4, 256, 256), BF16),
            pltpu.VMEM((4, 256, 256), BF16),
            pltpu.VMEM((2, 256, 256), BF16),
            pltpu.VMEM((3, 256, 256), BF16),
            pltpu.VMEM((256, 256), BF16),
            dma((5,)), dma((5,)), dma((4,)), dma((4,)),
            dma((16,)), dma((16,)), dma((16,)), dma((16,)), dma((16,)), dma((16,)),
            dma((4,)), dma((4,)), dma((4,)), dma((4,)),
            dma((4,)), dma((4,)), dma((5,)), dma((5,)),
        ],
        compiler_params=pltpu.CompilerParams(
            collective_id=0, has_side_effects=True, vmem_limit_bytes=63 * 1024 * 1024
        ),
    )(
        slot_requests, cache_lengths, page_table, frequency,
        span_tokens.reshape(256, 256), q_weight, kv_weight.T, out_weight, jnp.swapaxes(kv_pool, 1, 2),
    )
    return out.reshape(1, 256, 256)


def solution(mesh):
    placed = (
        P("group", "seq", "tensor"),
        P(None, "tensor"),
        P(None, "tensor"),
        P("tensor", None),
        P("group", None, "tensor"),
        P(),
        P(),
        P(),
    )
    return jax.shard_map(
        shards, mesh=mesh, in_specs=placed, out_specs=P("group", "seq", "tensor"), check_vma=False
    )
```

```python
import jax
import jax.numpy as jnp
import numpy as np
from jax import lax
from jax.experimental import pallas as pl
from jax.experimental.pallas import tpu as pltpu
from jax.sharding import PartitionSpec as P

HD = 64
WINDOW = 2048
PAGE = 128
MESH = pl.DeviceIdType.MESH
NEG = -1e30
FLOOR = -1e20
F32 = jnp.float32
BF16 = jnp.bfloat16


def layer_kernel(
    slots_ref, lengths_ref, table_ref, freq_hbm, x_hbm, qw_hbm, kvw_hbm, ow_hbm, pool_hbm,
    out_ref,
    x_ref, qw_ref, kvw_ref, ow_ref, pool_ref, freq_ref, place_ref, load_sem, xs, outp, kv, fresh, qacc, kvacc, qt, acc, top, tot, thr_ref, cos_ref, sin_ref, part, mine, pairin, bsum, landed, relay,
    x_send, x_recv, xf_send, xf_recv, p_send, p_recv, pf_send, pf_recv,
    n_send, n_recv, nf_send, nf_recv, r_send, r_recv, s_send, s_recv,
):
    group = lax.axis_index("group")
    seq = lax.axis_index("seq")
    tensor = lax.axis_index("tensor")
    chip = tensor // 2
    core = tensor % 2
    gy = group // 4
    gz = group % 4
    partner = {"tensor": chip * 2 + (1 - core)}

    def chip_at(d):
        return {"tensor": ((chip + d) % 4) * 2 + core}

    def group_to(s):
        dy, dz = s // 4, s % 4
        return ((gy + dy) % 4) * 4 + (gz + dz) % 4

    def group_from(s):
        dy, dz = s // 4, s % 4
        return ((gy - dy + 4) % 4) * 4 + (gz - dz + 4) % 4

    def page_dev(s):
        if s % 4 == 2:
            return {"group": group_to(s), "seq": seq + 1 - 2 * (seq % 2)}
        return {"group": group_to(s)}

    def remote(src, dst, ss, rs, dev):
        return pltpu.make_async_remote_copy(
            src_ref=src, dst_ref=dst, send_sem=ss, recv_sem=rs, device_id=dev, device_id_type=MESH
        )

    barrier = pltpu.get_barrier_semaphore()
    for s in range(1, 16):
        pl.semaphore_signal(barrier, inc=1, device_id=page_dev(s), device_id_type=MESH)
    for b in range(1, 4):
        pl.semaphore_signal(barrier, inc=1, device_id={"seq": (seq + b) % 4}, device_id_type=MESH)
    for d in range(1, 4):
        if d != 2:
            pl.semaphore_signal(barrier, inc=1, device_id=chip_at(d), device_id_type=MESH)
    pl.semaphore_signal(barrier, inc=1, device_id=partner, device_id_type=MESH)

    loads = [
        pltpu.make_async_copy(src, dst, load_sem.at[i])
        for i, (src, dst) in enumerate(
            [(pool_hbm, pool_ref), (x_hbm, x_ref), (qw_hbm, qw_ref), (kvw_hbm, kvw_ref), (ow_hbm, ow_ref), (freq_hbm, freq_ref)]
        )
    ]
    for copy in loads:
        copy.start()

    mine_req = slots_ref[group]
    length = lengths_ref[mine_req]
    loads[1].wait()
    pl.semaphore_wait(barrier, 21)

    fwd = 1 + 2 * core
    back = 3 - 2 * core
    halves = [pl.ds(0, 128), pl.ds(128, 128)]
    first = [
        remote(x_ref.at[half], xs.at[0, back, half], x_send.at[i], x_recv.at[i], chip_at(fwd))
        for i, half in enumerate(halves)
    ]
    first.append(remote(x_ref, xs.at[0, fwd], x_send.at[2], x_recv.at[2], chip_at(back)))
    own_x = remote(x_ref, xs.at[1, 0], xf_send.at[0], xf_recv.at[0], partner)
    for copy in first:
        copy.start()
    own_x.start()

    loads[0].wait()

    def pick(s, carry):
        req = slots_ref[group_to(s)]
        at = 0
        for w in range(16):
            off = table_ref[req, w] - group * 16
            at = at + jnp.where((off & -16) == 0, off, 0)
        outp[s] = pool_ref[at]
        return carry

    lax.fori_loop(0, 16, pick, 0)
    kv[core, 0] = outp[0]

    order = [1, 3, 4, 8, 12, 5, 7, 9, 11, 13, 15, 2, 6, 10, 14]
    pages = {
        s: remote(outp.at[s], kv.at[core, s], p_send.at[s], p_recv.at[s], page_dev(s)) for s in order
    }
    for s in (2, 6, 10, 14, 1, 3, 5, 7, 9, 11, 13, 15, 4, 8, 12):
        pages[s].start()
    pagef = {
        s: remote(kv.at[core, s], kv.at[core, s], pf_send.at[s], pf_recv.at[s], partner) for s in range(16)
    }
    pagef[0].start()

    loads[5].wait()
    at_pos = lax.broadcasted_iota(jnp.int32, (32, 256), 1) + (length + seq * 256)
    angles = at_pos.astype(F32) * freq_ref[...]
    cos = jnp.cos(angles)
    sin = jnp.sin(angles)
    cos_ref[...] = cos
    sin_ref[...] = sin
    thr_ref[...] = jnp.maximum(
        lax.broadcasted_iota(jnp.int32, (1, 256), 1) + seq * 256, WINDOW - 1 - length
    )
    for h in range(4):
        acc[h] = jnp.zeros((HD, 256), F32)
        top[h] = jnp.full((1, 256), FLOOR, F32)
        tot[h] = jnp.zeros((1, 256), F32)

    my_ids = [table_ref[mine_req, w] for w in range(16)]

    def find_place(s, carry):
        low = group_from(s) * 16
        at = 0
        for w in range(16):
            off = my_ids[w] - low
            at = at + jnp.where((off & -16) == 0, w, 0)
        place_ref[s] = at
        return carry

    lax.fori_loop(0, 16, find_place, 0)

    loads[2].wait()
    loads[3].wait()

    def project(p, d, start=False):
        block = x_ref[...] if start else xs[p, d]
        t = ((chip + d) % 4) * 2 + (core if p == 0 else 1 - core)
        rows = pl.ds(pl.multiple_of(t * 256, 256), 256)
        q = jnp.dot(block, qw_ref[rows, :], preferred_element_type=F32)
        f = lax.dot_general(kvw_ref[:, rows], block, (((1,), (1,)), ((), ())), preferred_element_type=F32)
        if start:
            qacc[...] = q
            kvacc[...] = f
        else:
            qacc[...] += q
            kvacc[...] += f

    def hand_over(i, d):
        return remote(xs.at[0, d], xs.at[1, d], xf_send.at[i], xf_recv.at[i], partner)

    project(0, 0, True)
    second = []
    for i, half in enumerate(halves):
        first[i].wait_recv()
        second.append(
            remote(xs.at[0, back, half], xs.at[0, 2, half], x_send.at[3 + i], x_recv.at[3 + i], chip_at(fwd))
        )
        second[i].start()
    xf = [hand_over(1, back), hand_over(3, fwd), hand_over(2, 2)]
    xf[0].start()
    own_x.wait_recv()
    project(1, 0)
    project(0, back)
    first[2].wait_recv()
    xf[1].start()
    project(0, fwd)
    hand_over(1, fwd).wait_recv()
    project(1, fwd)
    hand_over(3, back).wait_recv()
    project(1, back)
    second[0].wait_recv()
    second[1].wait_recv()
    xf[2].start()
    project(0, 2)
    xf[2].wait_recv()
    project(1, 2)

    is_key = jnp.where(core == 0, 1.0, 0.0).astype(F32)
    cos = cos_ref[...]
    sin = sin_ref[...]
    kcos = cos * is_key + (1.0 - is_key)
    ksin = sin * is_key
    a = kvacc[:32, :]
    b = kvacc[32:, :]
    fresh[core, 0] = jnp.concatenate([a * kcos - b * ksin, b * kcos + a * ksin], axis=0).astype(BF16)
    for step in range(1, 4):
        @pl.when(seq + step < 4)
        def _():
            remote(
                fresh.at[core, 0], fresh.at[core, step], n_send.at[step], n_recv.at[step], {"seq": (seq + step) % 4}
            ).start()
    newf = {
        i: remote(fresh.at[core, i], fresh.at[core, i], nf_send.at[i], nf_recv.at[i], partner) for i in range(4)
    }
    newf[0].start()
    for h in range(4):
        w = qacc[:, h * HD:(h + 1) * HD].T
        a = w[:32, :] * 0.125
        b = w[32:, :] * 0.125
        qt[h] = jnp.concatenate([a * cos - b * sin, b * cos + a * sin], axis=0).astype(BF16)

    def fold(keys, values, mask):
        kb = keys.T

        def head_pair(i, carry):
            scores = [jnp.dot(kb, qt[2 * i + k], preferred_element_type=F32) for k in range(2)]
            for k in range(2):
                h = 2 * i + k
                s = mask(scores[k])
                old = top[h]
                new = jnp.maximum(old, jnp.max(s, axis=0, keepdims=True))
                p = jnp.exp(s - new)
                alpha = jnp.exp(old - new)
                top[h] = new
                tot[h] = tot[h] * alpha + jnp.sum(p, axis=0, keepdims=True)
                acc[h] = acc[h] * alpha + jnp.dot(values, p.astype(BF16), preferred_element_type=F32)
            return carry

        lax.fori_loop(0, 2, head_pair, 0)

    row = lax.broadcasted_iota(jnp.int32, (PAGE, 256), 0)

    def fold_pages(slots):
        def mask(s):
            pieces = []
            for i, slot in enumerate(slots):
                low = thr_ref[...] - place_ref[slot] * PAGE
                pieces.append(jnp.where(row > low, s[i * PAGE:(i + 1) * PAGE], NEG))
            return jnp.concatenate(pieces, axis=0)

        fold(
            jnp.concatenate([kv[0, s] for s in slots], axis=1),
            jnp.concatenate([kv[1, s] for s in slots], axis=1),
            mask,
        )

    def take(slots):
        for s in slots:
            pages[s].wait_recv()
            pagef[s].start()

    def ready(slots):
        for s in slots:
            remote(kv.at[core, s], kv.at[1 - core, s], pf_send.at[s], pf_recv.at[s], partner).wait_recv()

    causal = lax.broadcasted_iota(jnp.int32, (256, 256), 0) <= lax.broadcasted_iota(jnp.int32, (256, 256), 1)

    def new_ready(i):
        remote(fresh.at[core, i], fresh.at[1 - core, i], nf_send.at[i], nf_recv.at[i], partner).wait_recv()

    take([4, 8, 12])
    new_ready(0)
    fold(fresh[0, 0], fresh[1, 0], lambda s: jnp.where(causal, s, NEG))
    c0, c1, c2, c3 = [0, 4, 8, 12], [1, 3, 5, 7], [9, 11, 13, 15], [2, 6, 10, 14]
    ready(c0)
    fold_pages(c0)
    take(c1)
    take(c2)
    ready(c1)
    fold_pages(c1)
    take(c3)
    ready(c2)
    fold_pages(c2)
    for step in range(1, 4):
        @pl.when(seq >= step)
        def _():
            remote(
                fresh.at[core, 0], fresh.at[core, step], n_send.at[step], n_recv.at[step], {"seq": (seq + step) % 4}
            ).wait_recv()
            newf[step].start()
    ready(c3)
    fold_pages(c3)
    for step in range(1, 4):
        @pl.when(seq >= step)
        def _():
            new_ready(step)
            fold(fresh[0, step], fresh[1, step], lambda s: s)

    loads[4].wait()
    heads = jnp.concatenate([(acc[h] / tot[h]).T.astype(BF16) for h in range(4)], axis=1)

    def partial_for(d, c):
        cols = pl.ds(pl.multiple_of((((chip + d) % 4) * 2 + c) * 256, 256), 256)
        return jnp.dot(heads, ow_ref[:, cols], preferred_element_type=F32).astype(BF16)

    near = 1 + 2 * core
    far = 3 - 2 * core
    up = {"tensor": ((chip + near) % 4) * 2 + core}
    down = {"tensor": ((chip + far) % 4) * 2 + core}
    rs = {}
    for d in (2, 1, 3, 0):
        part[d] = partial_for(d, 1 - core)
        rs[d] = remote(part.at[d], pairin.at[d], r_send.at[d], r_recv.at[d], partner)
        rs[d].start()
        if d == 2:
            mine[2] = partial_for(2, core)
    rs[2].wait_recv()
    s2, s1 = [], []
    for i, half in enumerate(halves):
        bsum[0, half] = (mine[2, half].astype(F32) + pairin[2, half].astype(F32)).astype(BF16)
        s2.append(remote(bsum.at[0, half], landed.at[0, half], s_send.at[i], s_recv.at[i], up))
        s2[i].start()
    mine[1] = partial_for(1, core)
    mine[3] = partial_for(3, core)
    rs[1].wait_recv()
    rs[3].wait_recv()
    bsum[1] = (mine[far].astype(F32) + pairin[far].astype(F32)).astype(BF16)
    s3 = remote(bsum.at[1], landed.at[1], s_send.at[2], s_recv.at[2], down)
    s3.start()
    mine[0] = partial_for(0, core)
    for i, half in enumerate(halves):
        nearsum = mine[near, half].astype(F32) + pairin[near, half].astype(F32)
        s2[i].wait_recv()
        relay[half] = (nearsum + landed[0, half].astype(F32)).astype(BF16)
        s1.append(remote(relay.at[half], landed.at[2, half], s_send.at[3 + i], s_recv.at[3 + i], up))
        s1[i].start()
    rs[0].wait_recv()
    s3.wait_recv()
    for i, half in enumerate(halves):
        total = mine[0, half].astype(F32) + pairin[0, half].astype(F32) + landed[1, half].astype(F32)
        s1[i].wait_recv()
        out_ref[half] = (total + landed[2, half].astype(F32)).astype(BF16)

    for copy in [*first, own_x, *second, *xf, *s1, *s2, s3]:
        copy.wait_send()
    for s in range(1, 16):
        pages[s].wait_send()
    for s in range(16):
        pagef[s].wait_send()
    for d in range(4):
        rs[d].wait_send()
    newf[0].wait_send()
    for step in range(1, 4):
        @pl.when(seq >= step)
        def _():
            newf[step].wait_send()

        @pl.when(seq + step < 4)
        def _():
            remote(
                fresh.at[core, 0], fresh.at[core, step], n_send.at[step], n_recv.at[step], {"seq": (seq + step) % 4}
            ).wait_send()


def shards(
    span_tokens, q_weight, kv_weight, out_weight, kv_pool, cache_lengths, slot_requests, page_table
):
    half_dim = HD // 2
    frequency = np.power(10000.0, -np.arange(half_dim) / half_dim).astype(np.float32)
    frequency = jnp.asarray(np.repeat(frequency[:, None], 256, axis=1))
    smem = pl.BlockSpec(memory_space=pltpu.SMEM)
    vmem = pl.BlockSpec(memory_space=pltpu.VMEM)
    hbm = pl.BlockSpec(memory_space=pl.ANY)
    dma = pltpu.SemaphoreType.DMA
    out = pl.pallas_call(
        layer_kernel,
        out_shape=jax.ShapeDtypeStruct((256, 256), BF16),
        in_specs=[smem] * 3 + [hbm] * 6,
        out_specs=vmem,
        scratch_shapes=[
            pltpu.VMEM((256, 256), BF16),
            pltpu.VMEM((2048, 256), BF16),
            pltpu.VMEM((HD, 2048), BF16),
            pltpu.VMEM((256, 2048), BF16),
            pltpu.VMEM((16, HD, PAGE), BF16),
            pltpu.VMEM((32, 256), F32),
            pltpu.SMEM((16,), jnp.int32),
            dma((6,)),
            pltpu.VMEM((2, 4, 256, 256), BF16),
            pltpu.VMEM((16, HD, PAGE), BF16),
            pltpu.VMEM((2, 16, HD, PAGE), BF16),
            pltpu.VMEM((2, 4, HD, 256), BF16),
            pltpu.VMEM((256, 256), F32),
            pltpu.VMEM((HD, 256), F32),
            pltpu.VMEM((4, HD, 256), BF16),
            pltpu.VMEM((4, HD, 256), F32),
            pltpu.VMEM((4, 1, 256), F32),
            pltpu.VMEM((4, 1, 256), F32),
            pltpu.VMEM((1, 256), jnp.int32),
            pltpu.VMEM((32, 256), F32),
            pltpu.VMEM((32, 256), F32),
            pltpu.VMEM((4, 256, 256), BF16),
            pltpu.VMEM((4, 256, 256), BF16),
            pltpu.VMEM((4, 256, 256), BF16),
            pltpu.VMEM((2, 256, 256), BF16),
            pltpu.VMEM((3, 256, 256), BF16),
            pltpu.VMEM((256, 256), BF16),
            dma((5,)), dma((5,)), dma((4,)), dma((4,)),
            dma((16,)), dma((16,)), dma((16,)), dma((16,)),
            dma((4,)), dma((4,)), dma((4,)), dma((4,)),
            dma((4,)), dma((4,)), dma((5,)), dma((5,)),
        ],
        compiler_params=pltpu.CompilerParams(
            collective_id=0, has_side_effects=True, vmem_limit_bytes=63 * 1024 * 1024
        ),
    )(
        slot_requests, cache_lengths, page_table, frequency,
        span_tokens.reshape(256, 256), q_weight, kv_weight.T, out_weight, jnp.swapaxes(kv_pool, 1, 2),
    )
    return out.reshape(1, 256, 256)


def solution(mesh):
    placed = (
        P("group", "seq", "tensor"),
        P(None, "tensor"),
        P(None, "tensor"),
        P("tensor", None),
        P("group", None, "tensor"),
        P(),
        P(),
        P(),
    )
    return jax.shard_map(
        shards, mesh=mesh, in_specs=placed, out_specs=P("group", "seq", "tensor"), check_vma=False
    )
```

```python
import jax
import jax.numpy as jnp
import numpy as np
from jax import lax
from jax.experimental import pallas as pl
from jax.experimental.pallas import tpu as pltpu
from jax.sharding import PartitionSpec as P

HD = 64
WINDOW = 2048
PAGE = 128
MESH = pl.DeviceIdType.MESH
NEG = -1e30
FLOOR = -1e20
F32 = jnp.float32
BF16 = jnp.bfloat16


def layer_kernel(
    slots_ref, lengths_ref, table_ref, freq_hbm, x_hbm, qw_hbm, kvw_hbm, ow_hbm, pool_hbm,
    out_ref,
    x_ref, qw_ref, kvw_ref, ow_ref, pool_ref, freq_ref, place_ref, load_sem, xs, outp, kv, fresh, qacc, kvacc, qt, acc, top, tot, thr_ref, cos_ref, sin_ref, part, mine, pairin, bsum, landed, relay,
    x_send, x_recv, xf_send, xf_recv, p_send, p_recv, pf_send, pf_recv,
    n_send, n_recv, nf_send, nf_recv, r_send, r_recv, s_send, s_recv,
):
    group = lax.axis_index("group")
    seq = lax.axis_index("seq")
    tensor = lax.axis_index("tensor")
    chip = tensor // 2
    core = tensor % 2
    gy = group // 4
    gz = group % 4
    partner = {"tensor": chip * 2 + (1 - core)}

    def chip_at(d):
        return {"tensor": ((chip + d) % 4) * 2 + core}

    def group_to(s):
        dy, dz = s // 4, s % 4
        return ((gy + dy) % 4) * 4 + (gz + dz) % 4

    def group_from(s):
        dy, dz = s // 4, s % 4
        return ((gy - dy + 4) % 4) * 4 + (gz - dz + 4) % 4

    def page_dev(s):
        if s % 4 == 2:
            return {"group": group_to(s), "seq": seq + 1 - 2 * (seq % 2)}
        return {"group": group_to(s)}

    def remote(src, dst, ss, rs, dev):
        return pltpu.make_async_remote_copy(
            src_ref=src, dst_ref=dst, send_sem=ss, recv_sem=rs, device_id=dev, device_id_type=MESH
        )

    barrier = pltpu.get_barrier_semaphore()
    for s in range(1, 16):
        pl.semaphore_signal(barrier, inc=1, device_id=page_dev(s), device_id_type=MESH)
    for b in range(1, 4):
        pl.semaphore_signal(barrier, inc=1, device_id={"seq": (seq + b) % 4}, device_id_type=MESH)
    for d in range(1, 4):
        if d != 2:
            pl.semaphore_signal(barrier, inc=1, device_id=chip_at(d), device_id_type=MESH)
    pl.semaphore_signal(barrier, inc=1, device_id=partner, device_id_type=MESH)

    loads = [
        pltpu.make_async_copy(src, dst, load_sem.at[i])
        for i, (src, dst) in enumerate(
            [(pool_hbm, pool_ref), (x_hbm, x_ref), (qw_hbm, qw_ref), (kvw_hbm, kvw_ref), (ow_hbm, ow_ref), (freq_hbm, freq_ref)]
        )
    ]
    for copy in loads:
        copy.start()

    mine_req = slots_ref[group]
    length = lengths_ref[mine_req]
    loads[0].wait()

    def pick(s, carry):
        req = slots_ref[group_to(s)]
        at = 0
        for w in range(16):
            off = table_ref[req, w] - group * 16
            at = at + jnp.where((off & -16) == 0, off, 0)
        outp[s] = pool_ref[at]
        return carry

    lax.fori_loop(0, 16, pick, 0)
    kv[core, 0] = outp[0]
    loads[1].wait()
    pl.semaphore_wait(barrier, 21)

    fwd = 1 + 2 * core
    back = 3 - 2 * core
    halves = [pl.ds(0, 128), pl.ds(128, 128)]
    first = [
        remote(x_ref.at[half], xs.at[0, back, half], x_send.at[i], x_recv.at[i], chip_at(fwd))
        for i, half in enumerate(halves)
    ]
    first.append(remote(x_ref, xs.at[0, fwd], x_send.at[2], x_recv.at[2], chip_at(back)))
    own_x = remote(x_ref, xs.at[1, 0], xf_send.at[0], xf_recv.at[0], partner)
    for copy in first:
        copy.start()
    own_x.start()
    order = [1, 3, 4, 8, 12, 5, 7, 9, 11, 13, 15, 2, 6, 10, 14]
    pages = {
        s: remote(outp.at[s], kv.at[core, s], p_send.at[s], p_recv.at[s], page_dev(s)) for s in order
    }
    for s in (2, 6, 10, 14, 1, 3, 5, 7, 9, 11, 13, 15, 4, 8, 12):
        pages[s].start()
    pagef = {
        s: remote(kv.at[core, s], kv.at[core, s], pf_send.at[s], pf_recv.at[s], partner) for s in range(16)
    }
    pagef[0].start()

    loads[5].wait()
    at_pos = lax.broadcasted_iota(jnp.int32, (32, 256), 1) + (length + seq * 256)
    angles = at_pos.astype(F32) * freq_ref[...]
    cos = jnp.cos(angles)
    sin = jnp.sin(angles)
    cos_ref[...] = cos
    sin_ref[...] = sin
    thr_ref[...] = jnp.maximum(
        lax.broadcasted_iota(jnp.int32, (1, 256), 1) + seq * 256, WINDOW - 1 - length
    )
    for h in range(4):
        acc[h] = jnp.zeros((HD, 256), F32)
        top[h] = jnp.full((1, 256), FLOOR, F32)
        tot[h] = jnp.zeros((1, 256), F32)

    my_ids = [table_ref[mine_req, w] for w in range(16)]

    def find_place(s, carry):
        low = group_from(s) * 16
        at = 0
        for w in range(16):
            off = my_ids[w] - low
            at = at + jnp.where((off & -16) == 0, w, 0)
        place_ref[s] = at
        return carry

    lax.fori_loop(0, 16, find_place, 0)

    loads[2].wait()
    loads[3].wait()

    def project(p, d, start=False):
        block = x_ref[...] if start else xs[p, d]
        t = ((chip + d) % 4) * 2 + (core if p == 0 else 1 - core)
        rows = pl.ds(pl.multiple_of(t * 256, 256), 256)
        q = jnp.dot(block, qw_ref[rows, :], preferred_element_type=F32)
        f = lax.dot_general(kvw_ref[:, rows], block, (((1,), (1,)), ((), ())), preferred_element_type=F32)
        if start:
            qacc[...] = q
            kvacc[...] = f
        else:
            qacc[...] += q
            kvacc[...] += f

    def hand_over(i, d):
        return remote(xs.at[0, d], xs.at[1, d], xf_send.at[i], xf_recv.at[i], partner)

    project(0, 0, True)
    second = []
    for i, half in enumerate(halves):
        first[i].wait_recv()
        second.append(
            remote(xs.at[0, back, half], xs.at[0, 2, half], x_send.at[3 + i], x_recv.at[3 + i], chip_at(fwd))
        )
        second[i].start()
    xf = [hand_over(1, back), hand_over(3, fwd), hand_over(2, 2)]
    xf[0].start()
    own_x.wait_recv()
    project(1, 0)
    project(0, back)
    first[2].wait_recv()
    xf[1].start()
    project(0, fwd)
    hand_over(1, fwd).wait_recv()
    project(1, fwd)
    hand_over(3, back).wait_recv()
    project(1, back)
    second[0].wait_recv()
    second[1].wait_recv()
    xf[2].start()
    project(0, 2)
    xf[2].wait_recv()
    project(1, 2)

    is_key = jnp.where(core == 0, 1.0, 0.0).astype(F32)
    cos = cos_ref[...]
    sin = sin_ref[...]
    kcos = cos * is_key + (1.0 - is_key)
    ksin = sin * is_key
    a = kvacc[:32, :]
    b = kvacc[32:, :]
    fresh[core, 0] = jnp.concatenate([a * kcos - b * ksin, b * kcos + a * ksin], axis=0).astype(BF16)
    for step in range(1, 4):
        @pl.when(seq + step < 4)
        def _():
            remote(
                fresh.at[core, 0], fresh.at[core, step], n_send.at[step], n_recv.at[step], {"seq": (seq + step) % 4}
            ).start()
    newf = {
        i: remote(fresh.at[core, i], fresh.at[core, i], nf_send.at[i], nf_recv.at[i], partner) for i in range(4)
    }
    newf[0].start()
    for h in range(4):
        w = qacc[:, h * HD:(h + 1) * HD].T
        a = w[:32, :] * 0.125
        b = w[32:, :] * 0.125
        qt[h] = jnp.concatenate([a * cos - b * sin, b * cos + a * sin], axis=0).astype(BF16)

    def fold(keys, values, mask):
        kb = keys.T
        summed = jnp.concatenate([values, jnp.ones((16, values.shape[1]), BF16)], axis=0)

        def head_pair(i, carry):
            scores = [jnp.dot(kb, qt[2 * i + k], preferred_element_type=F32) for k in range(2)]
            for k in range(2):
                h = 2 * i + k
                s = mask(scores[k])
                old = top[h]
                new = jnp.maximum(old, jnp.max(s, axis=0, keepdims=True))
                p = jnp.exp(s - new)
                alpha = jnp.exp(old - new)
                top[h] = new
                mixed = jnp.dot(summed, p.astype(BF16), preferred_element_type=F32)
                tot[h] = tot[h] * alpha + mixed[HD:HD + 1]
                acc[h] = acc[h] * alpha + mixed[:HD]
            return carry

        lax.fori_loop(0, 2, head_pair, 0)

    row = lax.broadcasted_iota(jnp.int32, (PAGE, 256), 0)

    def fold_pages(slots):
        def mask(s):
            pieces = []
            for i, slot in enumerate(slots):
                low = thr_ref[...] - place_ref[slot] * PAGE
                pieces.append(jnp.where(row > low, s[i * PAGE:(i + 1) * PAGE], NEG))
            return jnp.concatenate(pieces, axis=0)

        fold(
            jnp.concatenate([kv[0, s] for s in slots], axis=1),
            jnp.concatenate([kv[1, s] for s in slots], axis=1),
            mask,
        )

    def take(slots):
        for s in slots:
            pages[s].wait_recv()
            pagef[s].start()

    def ready(slots):
        for s in slots:
            remote(kv.at[core, s], kv.at[1 - core, s], pf_send.at[s], pf_recv.at[s], partner).wait_recv()

    causal = lax.broadcasted_iota(jnp.int32, (256, 256), 0) <= lax.broadcasted_iota(jnp.int32, (256, 256), 1)

    def new_ready(i):
        remote(fresh.at[core, i], fresh.at[1 - core, i], nf_send.at[i], nf_recv.at[i], partner).wait_recv()

    take([4, 8, 12])
    new_ready(0)
    fold(fresh[0, 0], fresh[1, 0], lambda s: jnp.where(causal, s, NEG))
    c0, c1, c2, c3 = [0, 4, 8, 12], [1, 3, 5, 7], [9, 11, 13, 15], [2, 6, 10, 14]
    ready(c0)
    fold_pages(c0)
    take(c1)
    take(c2)
    ready(c1)
    fold_pages(c1)
    take(c3)
    ready(c2)
    fold_pages(c2)
    for step in range(1, 4):
        @pl.when(seq >= step)
        def _():
            remote(
                fresh.at[core, 0], fresh.at[core, step], n_send.at[step], n_recv.at[step], {"seq": (seq + step) % 4}
            ).wait_recv()
            newf[step].start()
    ready(c3)
    fold_pages(c3)
    for step in range(1, 4):
        @pl.when(seq >= step)
        def _():
            new_ready(step)
            fold(fresh[0, step], fresh[1, step], lambda s: s)

    loads[4].wait()
    heads = jnp.concatenate([(acc[h] / tot[h]).T.astype(BF16) for h in range(4)], axis=1)

    def partial_for(d, c):
        cols = pl.ds(pl.multiple_of((((chip + d) % 4) * 2 + c) * 256, 256), 256)
        return jnp.dot(heads, ow_ref[:, cols], preferred_element_type=F32).astype(BF16)

    near = 1 + 2 * core
    far = 3 - 2 * core
    up = {"tensor": ((chip + near) % 4) * 2 + core}
    down = {"tensor": ((chip + far) % 4) * 2 + core}
    rs = {}
    for d in (2, 1, 3, 0):
        part[d] = partial_for(d, 1 - core)
        rs[d] = remote(part.at[d], pairin.at[d], r_send.at[d], r_recv.at[d], partner)
        rs[d].start()
        if d == 2:
            mine[2] = partial_for(2, core)
    rs[2].wait_recv()
    s2, s1 = [], []
    for i, half in enumerate(halves):
        bsum[0, half] = (mine[2, half].astype(F32) + pairin[2, half].astype(F32)).astype(BF16)
        s2.append(remote(bsum.at[0, half], landed.at[0, half], s_send.at[i], s_recv.at[i], up))
        s2[i].start()
    mine[1] = partial_for(1, core)
    mine[3] = partial_for(3, core)
    rs[1].wait_recv()
    rs[3].wait_recv()
    bsum[1] = (mine[far].astype(F32) + pairin[far].astype(F32)).astype(BF16)
    s3 = remote(bsum.at[1], landed.at[1], s_send.at[2], s_recv.at[2], down)
    s3.start()
    mine[0] = partial_for(0, core)
    for i, half in enumerate(halves):
        nearsum = mine[near, half].astype(F32) + pairin[near, half].astype(F32)
        s2[i].wait_recv()
        relay[half] = (nearsum + landed[0, half].astype(F32)).astype(BF16)
        s1.append(remote(relay.at[half], landed.at[2, half], s_send.at[3 + i], s_recv.at[3 + i], up))
        s1[i].start()
    rs[0].wait_recv()
    s3.wait_recv()
    for i, half in enumerate(halves):
        total = mine[0, half].astype(F32) + pairin[0, half].astype(F32) + landed[1, half].astype(F32)
        s1[i].wait_recv()
        out_ref[half] = (total + landed[2, half].astype(F32)).astype(BF16)

    for copy in [*first, own_x, *second, *xf, *s1, *s2, s3]:
        copy.wait_send()
    for s in range(1, 16):
        pages[s].wait_send()
    for s in range(16):
        pagef[s].wait_send()
    for d in range(4):
        rs[d].wait_send()
    newf[0].wait_send()
    for step in range(1, 4):
        @pl.when(seq >= step)
        def _():
            newf[step].wait_send()

        @pl.when(seq + step < 4)
        def _():
            remote(
                fresh.at[core, 0], fresh.at[core, step], n_send.at[step], n_recv.at[step], {"seq": (seq + step) % 4}
            ).wait_send()


def shards(
    span_tokens, q_weight, kv_weight, out_weight, kv_pool, cache_lengths, slot_requests, page_table
):
    half_dim = HD // 2
    frequency = np.power(10000.0, -np.arange(half_dim) / half_dim).astype(np.float32)
    frequency = jnp.asarray(np.repeat(frequency[:, None], 256, axis=1))
    smem = pl.BlockSpec(memory_space=pltpu.SMEM)
    vmem = pl.BlockSpec(memory_space=pltpu.VMEM)
    hbm = pl.BlockSpec(memory_space=pl.ANY)
    dma = pltpu.SemaphoreType.DMA
    out = pl.pallas_call(
        layer_kernel,
        out_shape=jax.ShapeDtypeStruct((256, 256), BF16),
        in_specs=[smem] * 3 + [hbm] * 6,
        out_specs=vmem,
        scratch_shapes=[
            pltpu.VMEM((256, 256), BF16),
            pltpu.VMEM((2048, 256), BF16),
            pltpu.VMEM((HD, 2048), BF16),
            pltpu.VMEM((256, 2048), BF16),
            pltpu.VMEM((16, HD, PAGE), BF16),
            pltpu.VMEM((32, 256), F32),
            pltpu.SMEM((16,), jnp.int32),
            dma((6,)),
            pltpu.VMEM((2, 4, 256, 256), BF16),
            pltpu.VMEM((16, HD, PAGE), BF16),
            pltpu.VMEM((2, 16, HD, PAGE), BF16),
            pltpu.VMEM((2, 4, HD, 256), BF16),
            pltpu.VMEM((256, 256), F32),
            pltpu.VMEM((HD, 256), F32),
            pltpu.VMEM((4, HD, 256), BF16),
            pltpu.VMEM((4, HD, 256), F32),
            pltpu.VMEM((4, 1, 256), F32),
            pltpu.VMEM((4, 1, 256), F32),
            pltpu.VMEM((1, 256), jnp.int32),
            pltpu.VMEM((32, 256), F32),
            pltpu.VMEM((32, 256), F32),
            pltpu.VMEM((4, 256, 256), BF16),
            pltpu.VMEM((4, 256, 256), BF16),
            pltpu.VMEM((4, 256, 256), BF16),
            pltpu.VMEM((2, 256, 256), BF16),
            pltpu.VMEM((3, 256, 256), BF16),
            pltpu.VMEM((256, 256), BF16),
            dma((5,)), dma((5,)), dma((4,)), dma((4,)),
            dma((16,)), dma((16,)), dma((16,)), dma((16,)),
            dma((4,)), dma((4,)), dma((4,)), dma((4,)),
            dma((4,)), dma((4,)), dma((5,)), dma((5,)),
        ],
        compiler_params=pltpu.CompilerParams(
            collective_id=0, has_side_effects=True, vmem_limit_bytes=63 * 1024 * 1024
        ),
    )(
        slot_requests, cache_lengths, page_table, frequency,
        span_tokens.reshape(256, 256), q_weight, kv_weight.T, out_weight, jnp.swapaxes(kv_pool, 1, 2),
    )
    return out.reshape(1, 256, 256)


def solution(mesh):
    placed = (
        P("group", "seq", "tensor"),
        P(None, "tensor"),
        P(None, "tensor"),
        P("tensor", None),
        P("group", None, "tensor"),
        P(),
        P(),
        P(),
    )
    return jax.shard_map(
        shards, mesh=mesh, in_specs=placed, out_specs=P("group", "seq", "tensor"), check_vma=False
    )
```
